1024 devices in a mesh: tok: 64 (over x, y, core), head: 16 (over z).
Axes of the slice: x: 4, y: 8, z: 16, core: 2. Of those that a mesh axis runs over, the one named last changes fastest.
Arguments:
- query_latent: bfloat16 [8192, 128, 512], P('tok', 'head'), may hold values from -100 to 100
- query_rotary: bfloat16 [8192, 8192], P('tok', 'head'), may hold values from -6 to 6
- latents: bfloat16 [8192, 512], P('tok'), may hold values from -8 to 8
- key_rotary: bfloat16 [8192, 64], P('tok'), may hold values from -6 to 6
- out_grad: bfloat16 [8192, 128, 512], P('tok', 'head'), may hold values from -6 to 6
- doc_lengths: int32 [33], replicated, may hold values from 1 to 384, 8192 in all
Outputs:
- grad_query_latent: bfloat16 [8192, 128, 512], P('tok', 'head')
- grad_query_rotary: bfloat16 [8192, 8192], P('tok', 'head')
- grad_latents: bfloat16 [8192, 512], P(('tok', 'head'))
- grad_key_rotary: bfloat16 [8192, 64], P(('tok', 'head'))
The draws below stay inside these ranges and needn't reach their ends.
Inputs may be any that keep to these rules, and one draw needn't show every extreme that they name: `doc_lengths`: the lengths sum to 8192, and some document has exactly 384 tokens.
All inputs are finite; a program needn't handle non-finite values.
Results may differ from the reference program's by a relative error of at most 0.013.
Values may be sent and summed in bfloat16 or wider, within the bound.
No kernel may reach another device: no remote copies, remote signals or barrier semaphores. Data moves between devices by JAX's collectives and lax.ppermute only.
A program may use at most 32 MiB of HBM per device.

```python
import math
import jax
import jax.numpy as jnp
import numpy as np
from jax import lax

HEADS = 128
DL = 512
DR = 64
TOK_DEV = 128
SPAN = 3
TOKENS = 8192
MAX_DOC = 384
DOCS = 33


def latent_base(key):
    raw = jnp.clip(jax.random.normal(jax.random.fold_in(key, 101), (TOKENS, DL), jnp.float32), -6.0, 6.0)
    return raw


def draw_latents(key, part):
    return latent_base(key).astype(jnp.bfloat16)


def draw_query_latent(key, part):
    noise = jnp.clip(jax.random.normal(jax.random.fold_in(key, 202), (TOKENS, HEADS, DL), jnp.float32), -6.0, 6.0)
    return noise.astype(jnp.bfloat16)


def level_of(key, dims, split, smallest, high):
    def one(position, blocks):
        steps = jax.random.uniform(jax.random.fold_in(jax.random.fold_in(key, 6), position), (blocks,), jnp.float32, smallest / len(split), high / len(split))
        return jnp.repeat(jnp.exp(steps), dims[position] // blocks).reshape((-1,) + (1,) * (len(dims) - position - 1))

    gain = one(*split[0])
    for cut in split[1:]:
        gain = gain * one(*cut)
    return gain


def profile(number_of, total, most, lean):
    loads = [(1 << 20) // math.isqrt(standing ** lean) + 1 for standing in range(2, number_of + 1)]
    rest, given = total - most - (number_of - 1), [1] * (number_of - 1)
    while rest > 0:
        free = [i for i in range(number_of - 1) if given[i] < most]
        mass, budget = sum([loads[i] for i in free]), rest
        for i in free:
            extra = min(most - given[i], max(1, budget * loads[i] // mass), rest)
            given[i] = given[i] + extra
            rest = rest - extra
    return np.array([most] + given)


def ragged_sizes(rng, amount, total, most, lean):
    if amount == 2:
        one = jax.random.randint(rng, (), max(1, total - most), min(most, total - 1) + 1)
        return jnp.stack([one, total - one])
    lengths = jnp.asarray(profile(amount, total, most, lean), jnp.int32)
    twos = (amount - 1) // 2
    giver, receiver = lengths[1:1 + 2 * twos:2], lengths[2:2 + 2 * twos:2]
    margin = jnp.minimum(giver - 1, most - receiver)
    moved = jax.random.randint(jax.random.fold_in(rng, 1), (twos,), 0, 1 << 20) % (margin + 1)
    lengths = lengths.at[1:1 + 2 * twos:2].set(giver - moved).at[2:2 + 2 * twos:2].set(receiver + moved)
    return lengths[jax.random.permutation(jax.random.fold_in(rng, 2), amount)]


def scatter_about(stream_key, extent, width, most, cuts=(), held_as=jnp.bfloat16):
    drawn = width * jax.random.normal(stream_key, extent, jnp.float32)
    if cuts:
        drawn = drawn * level_of(stream_key, extent, cuts, -0.22, 0.18)
    return jnp.clip(drawn, -most, most).astype(held_as)


def setup_inputs(seed: int = 0) -> dict:
    streams_of = jax.random.split(jax.random.key(seed), 7)
    return {
        "query_latent": draw_query_latent(jax.random.fold_in(streams_of[6], 71), 0),
        "query_rotary": scatter_about(streams_of[1], (TOKENS, HEADS * DR), 1.0, 6.0, ((0, 64), (1, 16))),
        "latents": draw_latents(jax.random.fold_in(streams_of[6], 71), 0),
        "key_rotary": scatter_about(streams_of[3], (TOKENS, DR), 1.0, 6.0, ((0, 64),)),
        "out_grad": scatter_about(streams_of[4], (TOKENS, HEADS, DL), 1.0, 6.0, ((0, 64), (1, 16))),
        "doc_lengths": ragged_sizes(streams_of[5], DOCS, TOKENS, MAX_DOC, 2).astype(jnp.int32),
    }


SCALE = 0.07216878364870322
NEGATIVE = -1.0e30


def reference(query_latent, query_rotary, latents, key_rotary, out_grad, doc_lengths):
    reach = SPAN * TOK_DEV
    window = reach + TOK_DEV
    doc_starts = (jnp.cumsum(doc_lengths) - doc_lengths).astype(jnp.int32)
    positions = jnp.arange(TOKENS, dtype=jnp.int32)
    query_start = jnp.max(jnp.where(doc_starts[None, :] <= positions[:, None], doc_starts[None, :], 0), axis=1).astype(jnp.int32)
    latent_pad = jnp.concatenate([jnp.zeros((reach, DL), latents.dtype), latents], axis=0)
    rotary_pad = jnp.concatenate([jnp.zeros((reach, DR), key_rotary.dtype), key_rotary], axis=0)
    rotary_query = query_rotary.reshape(TOKENS, HEADS, DR)

    def one_block(carry, block_index):
        grad_latent_pad, grad_rotary_pad = carry
        first = (block_index * TOK_DEV).astype(jnp.int32)
        query_lat = lax.dynamic_slice_in_dim(query_latent, first, TOK_DEV, 0).astype(jnp.float32)
        query_rot = lax.dynamic_slice_in_dim(rotary_query, first, TOK_DEV, 0).astype(jnp.float32)
        grad_out = lax.dynamic_slice_in_dim(out_grad, first, TOK_DEV, 0).astype(jnp.float32)
        key_lat = lax.dynamic_slice_in_dim(latent_pad, first, window, 0).astype(jnp.float32)
        key_rot = lax.dynamic_slice_in_dim(rotary_pad, first, window, 0).astype(jnp.float32)
        query_pos = first + jnp.arange(TOK_DEV, dtype=jnp.int32)
        key_pos = first - reach + jnp.arange(window, dtype=jnp.int32)
        start_here = lax.dynamic_slice_in_dim(query_start, first, TOK_DEV, 0)
        visible = (key_pos[None, :] >= start_here[:, None]) & (key_pos[None, :] <= query_pos[:, None])
        scores = SCALE * (jnp.einsum("qhd,kd->hqk", query_lat, key_lat) + jnp.einsum("qhr,kr->hqk", query_rot, key_rot))
        masked = jnp.where(visible[None], scores, NEGATIVE)
        row_max = jnp.max(masked, axis=2, keepdims=True)
        exp_terms = jnp.where(visible[None], jnp.exp(masked - row_max), 0.0)
        attn_probs = exp_terms / jnp.sum(exp_terms, axis=2, keepdims=True)
        probs_low = lax.optimization_barrier(attn_probs.astype(jnp.bfloat16)).astype(jnp.float32)
        attn_out = jnp.einsum("hqk,kd->qhd", probs_low, key_lat)
        row_delta = jnp.sum(grad_out * attn_out, axis=2)
        prob_grad = jnp.einsum("qhd,kd->hqk", grad_out, key_lat)
        score_grad = attn_probs * (prob_grad - jnp.transpose(row_delta)[:, :, None])
        score_low = lax.optimization_barrier(score_grad.astype(jnp.bfloat16)).astype(jnp.float32)
        grad_query_lat = (SCALE * jnp.einsum("hqk,kd->qhd", score_low, key_lat)).astype(jnp.bfloat16)
        grad_query_rot = (SCALE * jnp.einsum("hqk,kr->qhr", score_low, key_rot)).reshape(TOK_DEV, HEADS * DR).astype(jnp.bfloat16)
        latent_term = SCALE * jnp.einsum("hqk,qhd->kd", score_low, query_lat) + jnp.einsum("hqk,qhd->kd", probs_low, grad_out)
        rotary_term = SCALE * jnp.einsum("hqk,qhr->kr", score_low, query_rot)
        grad_latent_pad = lax.dynamic_update_slice_in_dim(grad_latent_pad, lax.dynamic_slice_in_dim(grad_latent_pad, first, window, 0) + latent_term, first, 0)
        grad_rotary_pad = lax.dynamic_update_slice_in_dim(grad_rotary_pad, lax.dynamic_slice_in_dim(grad_rotary_pad, first, window, 0) + rotary_term, first, 0)
        return (grad_latent_pad, grad_rotary_pad), (grad_query_lat, grad_query_rot)

    initial = (jnp.zeros((TOKENS + reach, DL), jnp.float32), jnp.zeros((TOKENS + reach, DR), jnp.float32))
    blocks_all = jnp.arange(TOKENS // TOK_DEV, dtype=jnp.int32)
    totals, per_block = lax.scan(one_block, initial, blocks_all)
    grad_query_latent = per_block[0].reshape(TOKENS, HEADS, DL)
    grad_query_rotary = per_block[1].reshape(TOKENS, HEADS * DR)
    grad_latents = totals[0][reach:].astype(jnp.bfloat16)
    grad_key_rotary = totals[1][reach:].astype(jnp.bfloat16)
    return grad_query_latent, grad_query_rotary, grad_latents, grad_key_rotary
```

```python
import jax
import jax.numpy as jnp
from jax import lax
from jax.sharding import PartitionSpec as P

SPAN = 3


SCALE = 0.07216878364870322
NEGATIVE = -1e30


def shifted(block, axis, distance):
    devices = range(lax.axis_size(axis))
    route = [(i - distance, i) for i in devices if i - distance in devices]
    return lax.ppermute(block, axis, route)


def body(query_latent, query_rotary, latents, key_rotary, out_grad, doc_lengths):
    tok_rows, latent_width = latents.shape
    head_count = query_latent.shape[1]
    rotary_width = key_rotary.shape[1]
    head_devices = lax.axis_size("head")
    shard = lax.axis_index("tok")
    offsets = jnp.arange(tok_rows, dtype=jnp.int32)
    query_pos = shard * tok_rows + offsets
    doc_starts = jnp.cumsum(doc_lengths) - doc_lengths
    query_start = jnp.max(
        jnp.where(doc_starts[None, :] <= query_pos[:, None], doc_starts[None, :], 0), axis=1
    )
    own_keys = jnp.concatenate([latents, key_rotary], axis=1)
    key_tiles = [own_keys]
    place_tiles = [query_pos]
    for distance in range(1, SPAN + 1):
        key_tiles.append(shifted(own_keys, "tok", distance))
        place_tiles.append(query_pos - distance * tok_rows)
    keys = jnp.concatenate(key_tiles, axis=0)
    key_latent = keys[:, :latent_width]
    key_rot = keys[:, latent_width:]
    key_place = jnp.concatenate(place_tiles, axis=0)
    rotary_query = query_rotary.reshape(tok_rows, head_count, rotary_width)
    visible = (key_place[None, :] >= query_start[:, None]) & (
        key_place[None, :] <= query_pos[:, None]
    )
    scores = SCALE * (
        jnp.einsum("qhd,kd->hqk", query_latent, key_latent, preferred_element_type=jnp.float32)
        + jnp.einsum("qhr,kr->hqk", rotary_query, key_rot, preferred_element_type=jnp.float32)
    )
    masked = jnp.where(visible[None], scores, NEGATIVE)
    row_max = jnp.max(masked, axis=2, keepdims=True)
    exp_terms = jnp.where(visible[None], jnp.exp(masked - row_max), 0.0)
    attn_probs = exp_terms / jnp.sum(exp_terms, axis=2, keepdims=True)
    probs_low = attn_probs.astype(jnp.bfloat16)
    prob_grad = jnp.einsum("qhd,kd->hqk", out_grad, key_latent, preferred_element_type=jnp.float32)
    row_delta = jnp.sum(probs_low.astype(jnp.float32) * prob_grad, axis=2, keepdims=True)
    score_grad = (attn_probs * (prob_grad - row_delta)).astype(jnp.bfloat16)
    grad_query_latent = (
        SCALE
        * jnp.einsum("hqk,kd->qhd", score_grad, key_latent, preferred_element_type=jnp.float32)
    ).astype(jnp.bfloat16)
    grad_query_rotary = (
        (SCALE * jnp.einsum("hqk,kr->qhr", score_grad, key_rot, preferred_element_type=jnp.float32))
        .reshape(tok_rows, head_count * rotary_width)
        .astype(jnp.bfloat16)
    )
    latent_grad = SCALE * jnp.einsum(
        "hqk,qhd->kd", score_grad, query_latent, preferred_element_type=jnp.float32
    ) + jnp.einsum("hqk,qhd->kd", probs_low, out_grad, preferred_element_type=jnp.float32)
    rotary_grad = SCALE * jnp.einsum(
        "hqk,qhr->kr", score_grad, rotary_query, preferred_element_type=jnp.float32
    )
    key_grad = jnp.concatenate([latent_grad, rotary_grad], axis=1)
    total = key_grad[:tok_rows]
    for distance in range(1, SPAN + 1):
        piece = key_grad[distance * tok_rows : (distance + 1) * tok_rows].astype(jnp.bfloat16)
        total = total + shifted(piece, "tok", -distance).astype(jnp.float32)
    blocks = total.astype(jnp.bfloat16).reshape(head_devices, tok_rows // head_devices, -1)
    blocks = lax.all_to_all(blocks, "head", split_axis=0, concat_axis=0, tiled=True)
    summed = jnp.sum(blocks.astype(jnp.float32), axis=0).astype(jnp.bfloat16)
    return (
        grad_query_latent,
        grad_query_rotary,
        summed[:, :latent_width],
        summed[:, latent_width:],
    )


def solution(mesh):
    in_specs = (
        P("tok", "head", None),
        P("tok", "head"),
        P("tok", None),
        P("tok", None),
        P("tok", "head", None),
        P(),
    )
    out_specs = (
        P("tok", "head", None),
        P("tok", "head"),
        P(("tok", "head"), None),
        P(("tok", "head"), None),
    )
    return jax.shard_map(body, mesh=mesh, in_specs=in_specs, out_specs=out_specs, check_vma=False)
```

```python
import jax
import jax.numpy as jnp
from jax import lax
from jax.experimental import pallas as pl
from jax.experimental.pallas import tpu as pltpu
from jax.sharding import PartitionSpec as P

SPAN = 3


SCALE = 0.07216878364870322
LOG2_E = 1.4426950408889634
NEGATIVE = -1e30

TOK = 128
HEADS = 8
DL = 512
DR = 64
ROWS = TOK * HEADS
KEYS = (SPAN + 1) * TOK
FAR = SPAN * TOK
PACK = TOK + TOK * DR // DL
CHUNK = 256
HALF = KEYS // 2

F32 = jnp.float32
BF16 = jnp.bfloat16
VMEM = pltpu.MemorySpace.VMEM
SMEM = pltpu.MemorySpace.SMEM
HBM = pltpu.MemorySpace.HBM

NT = (((1,), (1,)), ((), ()))
NN = (((1,), (0,)), ((), ()))


def dot(a, b, dims):
    return lax.dot_general(a, b, dims, preferred_element_type=F32)


def spec(space=VMEM):
    return pl.BlockSpec(memory_space=space)


def store_rotary(ref, rotary_t):
    for i in range(DL // TOK):
        ref[TOK:PACK, i * TOK : (i + 1) * TOK] = rotary_t[16 * i : 16 * (i + 1), :].astype(ref.dtype)


def load_rotary(ref):
    parts = [ref[TOK:PACK, i * TOK : (i + 1) * TOK] for i in range(DL // TOK)]
    return jnp.concatenate(parts, axis=0)


def pack_kernel(lat_ref, rot_t_ref, out_ref, sems):
    copies = [pltpu.make_async_copy(lat_ref, out_ref.at[pl.ds(0, TOK), :], sems.at[0])]
    for i in range(DL // TOK):
        place = out_ref.at[pl.ds(TOK, PACK - TOK), pl.ds(i * TOK, TOK)]
        copies.append(
            pltpu.make_async_copy(rot_t_ref.at[pl.ds(16 * i, 16), :], place, sems.at[1 + i])
        )
    for copy in copies:
        copy.start()
    for copy in copies:
        copy.wait()


def pair_kernel(first_ref, second_ref, order_ref, out_ref):
    del order_ref
    out_ref[0:PACK, :] = first_ref[...]
    out_ref[PACK:, :] = second_ref[...]


def head_half(shape, head):
    lane = lax.broadcasted_iota(jnp.int32, shape, 1)
    return (lane >= DR) == (head % 2 == 1)


def rows_kernel(
    lens_ref, shard_ref, q_ref, do_ref, qr_ref, qv_ref, dov_ref, qx_ref, low_ref, qx32_ref, sems
):
    q_copy = pltpu.make_async_copy(q_ref, qv_ref, sems.at[0])
    do_copy = pltpu.make_async_copy(do_ref, dov_ref, sems.at[1])
    q_copy.start()
    do_copy.start()
    for head in range(HEADS):
        pair = qr_ref[:, (head // 2) * 2 * DR : (head // 2 + 1) * 2 * DR].astype(F32)
        qx32_ref[pl.ds(head, TOK, stride=HEADS), :] = jnp.where(
            head_half((TOK, 2 * DR), head), pair, 0.0
        )
    qx_ref[...] = qx32_ref[...].astype(BF16)
    high = lax.broadcasted_iota(jnp.int32, (1, ROWS), 1) // HEADS + FAR
    low = jnp.zeros((1, ROWS), jnp.int32)
    start = (SPAN - shard_ref[0]) * TOK
    for doc in range(lens_ref.shape[0]):
        low = jnp.where(high >= start, start, low)
        start = start + lens_ref[doc]
    low_ref[...] = low
    q_copy.wait()
    do_copy.wait()


def load_keys(ref, slot, keys_ref, rot2_ref):
    rows = slice(slot * TOK, (slot + 1) * TOK)
    keys_ref[rows, :] = ref[0:TOK, :]
    rot_t = load_rotary(ref).astype(F32)
    rot2_ref[rows, :] = jnp.transpose(jnp.concatenate([rot_t, rot_t], axis=0)).astype(BF16)


def near_kernel(
    q_ref, qx_ref, do_ref, own_ref, k2_ref, raw_ref, prob_grad_ref, keys_ref, rot2_ref
):
    load_keys(k2_ref, 0, keys_ref, rot2_ref)
    load_keys(own_ref, 1, keys_ref, rot2_ref)
    raw_ref[...] = dot(keys_ref[...], q_ref[...], NT) + dot(rot2_ref[...], qx_ref[...], NT)
    prob_grad_ref[...] = dot(keys_ref[...], do_ref[...], NT)


def scores_kernel(
    low_ref, q_ref, qx_ref, do_ref, k13_ref, raw_ref, prob_grad_ref, near_ref, near2_ref,
    f13_ref, dst_ref, pt_ref, keys_ref, rot2_ref,
):
    k1_ref = k13_ref.at[pl.ds(0, PACK), :]
    k3_ref = k13_ref.at[pl.ds(PACK, PACK), :]
    load_keys(k3_ref, 0, keys_ref, rot2_ref)
    load_keys(k1_ref, 1, keys_ref, rot2_ref)
    keys_ref[HALF:, :] = near_ref[...]
    rot2_ref[HALF:, :] = near2_ref[...]
    low = low_ref[...]
    high = lax.broadcasted_iota(jnp.int32, (1, ROWS), 1) // HEADS + FAR
    key = lax.broadcasted_iota(jnp.int32, (TOK, CHUNK), 0)
    far = slice(0, HALF)
    for c in range(ROWS // CHUNK):
        cols = slice(c * CHUNK, (c + 1) * CHUNK)
        raw_far = dot(keys_ref[far, :], q_ref[cols, :], NT) + dot(rot2_ref[far, :], qx_ref[cols, :], NT)
        lower = low[:, cols]
        masked = jnp.concatenate(
            [
                jnp.where(key >= lower, raw_far[0:TOK], NEGATIVE),
                jnp.where(key >= lower - 2 * TOK, raw_far[TOK:], NEGATIVE),
                jnp.where(key >= lower - TOK, raw_ref[0:TOK, cols], NEGATIVE),
                jnp.where(
                    (key >= lower - FAR) & (key <= high[:, cols] - FAR), raw_ref[TOK:, cols], NEGATIVE
                ),
            ],
            axis=0,
        )
        peak = jnp.max(masked, axis=0, keepdims=True)
        terms = jnp.exp2((masked - peak) * (SCALE * LOG2_E))
        probs = terms * (1.0 / jnp.sum(terms, axis=0, keepdims=True))
        low_probs = probs.astype(BF16)
        pt_ref[:, cols] = low_probs
        prob_grad = jnp.concatenate(
            [dot(keys_ref[far, :], do_ref[cols, :], NT), prob_grad_ref[:, cols]], axis=0
        )
        delta = jnp.sum(low_probs.astype(F32) * prob_grad, axis=0, keepdims=True)
        dst_ref[:, cols] = (probs * (prob_grad - delta)).astype(BF16)

    grad = SCALE * dot(dst_ref[far, :], q_ref[...], NN) + dot(pt_ref[far, :], do_ref[...], NN)
    rot = SCALE * dot(dst_ref[far, :], qx_ref[...], NN)
    store_tile(f13_ref.at[pl.ds(PACK, PACK), :], grad[0:TOK, :], rot[0:TOK, :])
    store_tile(f13_ref.at[pl.ds(0, PACK), :], grad[TOK:, :], rot[TOK:, :])


def fold_rotary(rot):
    rot_t = jnp.transpose(rot)
    return rot_t[0:DR, :] + rot_t[DR:, :]


def store_tile(ref, grad, rot):
    ref[0:TOK, :] = grad.astype(ref.dtype)
    store_rotary(ref, fold_rotary(rot))


def near_grads_kernel(q_ref, qx_ref, do_ref, dst_ref, pt_ref, f2_ref, g0_ref):
    near = slice(HALF, KEYS)
    grad = SCALE * dot(dst_ref[near, :], q_ref[...], NN) + dot(pt_ref[near, :], do_ref[...], NN)
    rot = SCALE * dot(dst_ref[near, :], qx_ref[...], NN)
    store_tile(f2_ref, grad[0:TOK, :], rot[0:TOK, :])
    store_tile(g0_ref, grad[TOK:, :], rot[TOK:, :])


def queries_kernel(dst_ref, keys_ref, rot2_ref, dq_ref, dqr_ref, x_ref):
    for c in range(ROWS // CHUNK):
        cols = slice(c * CHUNK, (c + 1) * CHUNK)
        ds = jnp.transpose(dst_ref[:, cols])
        dq_ref[cols, :] = (SCALE * dot(ds, keys_ref[...], NN)).astype(BF16)
        x_ref[cols, :] = SCALE * dot(ds, rot2_ref[...], NN)
    for pair in range(HEADS // 2):
        even = x_ref[pl.ds(2 * pair, TOK, stride=HEADS), :]
        odd = x_ref[pl.ds(2 * pair + 1, TOK, stride=HEADS), :]
        dqr_ref[:, pair * 2 * DR : (pair + 1) * 2 * DR] = jnp.where(
            head_half((TOK, 2 * DR), 0), even, odd
        ).astype(BF16)


def relay_kernel(f2_ref, r13_ref, out_ref):
    out_ref[...] = (f2_ref[...] + r13_ref[PACK:, :].astype(F32)).astype(BF16)


def total_kernel(g0_ref, r13_ref, r2_ref, out_ref):
    total = g0_ref[...] + r13_ref[0:PACK, :].astype(F32) + r2_ref[...].astype(F32)
    out_ref[:, 0:DL] = total[0:TOK, :].astype(BF16)
    parts = [total[TOK:, i * TOK : (i + 1) * TOK] for i in range(DL // TOK)]
    rot = jnp.transpose(jnp.concatenate(parts + parts, axis=0))
    out_ref[:, DL:] = rot[:, 0:DR].astype(BF16)


def sum_kernel(blocks_ref, lat_ref, rot_ref):
    total = jnp.sum(blocks_ref[...].astype(F32), axis=0)
    lat_ref[...] = total[:, 0:DL].astype(BF16)
    rot_ref[...] = total[:, DL:].astype(BF16)


def shape(dims, dtype=BF16):
    return jax.ShapeDtypeStruct(dims, dtype)


def call(kernel, outs, spaces, scratch=(), flops=0, moved=0, name=None, limit=24):
    return pl.pallas_call(
        kernel,
        out_shape=outs,
        in_specs=[spec(s) for s in spaces],
        out_specs=jax.tree.map(lambda _: spec(), outs),
        scratch_shapes=scratch,
        compiler_params=pltpu.CompilerParams(vmem_limit_bytes=limit << 20),
        cost_estimate=pl.CostEstimate(flops=flops, bytes_accessed=moved, transcendentals=0),
        name=name,
    )


def pack(latents, rotary_t):
    return call(
        pack_kernel, shape((PACK, DL)), [HBM] * 2,
        scratch=[pltpu.SemaphoreType.DMA((1 + DL // TOK,))], moved=300000, name="pack",
    )(latents, rotary_t)


def pair_up(first, second, order):
    return call(pair_kernel, shape((2 * PACK, DL)), [VMEM] * 3, moved=600000, name="pair")(
        first, second, order
    )


def row_setup(lens, shard, q, do, qr):
    outs = (shape((ROWS, DL)), shape((ROWS, DL)), shape((ROWS, 2 * DR)), shape((1, ROWS), jnp.int32))
    return call(
        rows_kernel, outs, [SMEM, SMEM, HBM, HBM, VMEM],
        scratch=[pltpu.VMEM((ROWS, 2 * DR), F32), pltpu.SemaphoreType.DMA((2,))],
        moved=4 << 20, name="row_setup",
    )(lens, shard, q, do, qr)


def near_scores(q, qx, do, own, k2):
    outs = (
        shape((HALF, ROWS), F32), shape((HALF, ROWS), F32), shape((HALF, DL)), shape((HALF, 2 * DR)),
    )
    return call(
        near_kernel, outs, [VMEM] * 5, flops=2 * ROWS * KEYS * DL, moved=4 << 20, name="near_scores"
    )(q, qx, do, own, k2)


def scores(low, q, qx, do, k13, raw, prob_grad, near, near2):
    outs = (
        shape((2 * PACK, DL)), shape((KEYS, ROWS)), shape((KEYS, ROWS)),
        shape((KEYS, DL)), shape((KEYS, 2 * DR)),
    )
    return call(
        scores_kernel, outs, [VMEM] * 9,
        flops=2 * ROWS * KEYS * DL * 2, moved=6 << 20, name="scores",
    )(low, q, qx, do, k13, raw, prob_grad, near, near2)


def near_grads(q, qx, do, dst, pt):
    tile = shape((PACK, DL), F32)
    return call(
        near_grads_kernel, (tile, tile), [VMEM] * 5,
        flops=2 * ROWS * KEYS * DL, moved=4 << 20, name="near_grads",
    )(q, qx, do, dst, pt)


def queries(dst, keys, rot2):
    outs = (shape((ROWS, DL)), shape((TOK, HEADS * DR)))
    return call(
        queries_kernel, outs, [VMEM] * 3, scratch=[pltpu.VMEM((ROWS, 2 * DR), F32)],
        flops=2 * ROWS * KEYS * DL, moved=4 << 20, name="queries",
    )(dst, keys, rot2)


def relay(f2, r13):
    return call(relay_kernel, shape((PACK, DL)), [VMEM] * 2, moved=600000, name="relay")(f2, r13)


def total(g0, r13, r2):
    return call(total_kernel, shape((TOK, DL + DR)), [VMEM] * 3, moved=1 << 20, name="total")(
        g0, r13, r2
    )


def head_sum(blocks):
    rows = blocks.shape[1]
    return call(
        sum_kernel, (shape((rows, DL)), shape((rows, DR))), [VMEM], moved=200000, name="head_sum"
    )(blocks)


def shifted(block, axis, distance):
    devices = range(lax.axis_size(axis))
    route = [(i - distance, i) for i in devices if i - distance in devices]
    return lax.ppermute(block, axis, route)


def body(query_latent, query_rotary, latents, key_rotary, out_grad, doc_lengths):
    head_devices = lax.axis_size("head")
    shard = jnp.reshape(lax.axis_index("tok"), (1,)).astype(jnp.int32)
    q = query_latent.reshape(ROWS, DL)
    do = out_grad.reshape(ROWS, DL)
    own = pack(latents, key_rotary.T)
    k2 = shifted(own, "tok", 2)
    q, do, qx, low = row_setup(doc_lengths, shard, q, do, query_rotary)
    k13 = shifted(pair_up(own, k2, low), "tok", 1)
    raw, prob_grad, near, near2 = near_scores(q, qx, do, own, k2)
    f13, dst, pt, keys, rot2 = scores(low, q, qx, do, k13, raw, prob_grad, near, near2)
    r13 = shifted(f13, "tok", -1)
    f2, g0 = near_grads(q, qx, do, dst, pt)
    r2 = shifted(relay(f2, r13), "tok", -2)
    dq, dqr = queries(dst, keys, rot2)
    blocks = total(g0, r13, r2).reshape(head_devices, TOK // head_devices, DL + DR)
    blocks = lax.all_to_all(blocks, "head", split_axis=0, concat_axis=0, tiled=True)
    grad_latents, grad_key_rotary = head_sum(blocks)
    return dq.reshape(TOK, HEADS, DL), dqr, grad_latents, grad_key_rotary


def solution(mesh):
    in_specs = (
        P("tok", "head", None),
        P("tok", "head"),
        P("tok", None),
        P("tok", None),
        P("tok", "head", None),
        P(),
    )
    out_specs = (
        P("tok", "head", None),
        P("tok", "head"),
        P(("tok", "head"), None),
        P(("tok", "head"), None),
    )
    return jax.shard_map(body, mesh=mesh, in_specs=in_specs, out_specs=out_specs, check_vma=False)
```

```python
import jax
import jax.numpy as jnp
from jax import lax
from jax.experimental import pallas as pl
from jax.experimental.pallas import tpu as pltpu
from jax.sharding import PartitionSpec as P

SPAN = 3


SCALE = 0.07216878364870322
LOG2_E = 1.4426950408889634
NEGATIVE = -1e30

TOK = 128
HEADS = 8
DL = 512
DR = 64
ROWS = TOK * HEADS
KEYS = (SPAN + 1) * TOK
FAR = SPAN * TOK
PACK = TOK + TOK * DR // DL
CHUNK = 256
HALF = KEYS // 2

F32 = jnp.float32
BF16 = jnp.bfloat16
VMEM = pltpu.MemorySpace.VMEM
SMEM = pltpu.MemorySpace.SMEM
HBM = pltpu.MemorySpace.HBM

NT = (((1,), (1,)), ((), ()))
NN = (((1,), (0,)), ((), ()))


def dot(a, b, dims):
    return lax.dot_general(a, b, dims, preferred_element_type=F32)


def spec(space=VMEM):
    return pl.BlockSpec(memory_space=space)


def store_rotary(ref, rotary_t):
    for i in range(DL // TOK):
        ref[TOK:PACK, i * TOK : (i + 1) * TOK] = rotary_t[16 * i : 16 * (i + 1), :].astype(ref.dtype)


def load_rotary(ref):
    parts = [ref[TOK:PACK, i * TOK : (i + 1) * TOK] for i in range(DL // TOK)]
    return jnp.concatenate(parts, axis=0)


def pack_kernel(lat_ref, rot_t_ref, out_ref, sems):
    copies = [pltpu.make_async_copy(lat_ref, out_ref.at[pl.ds(0, TOK), :], sems.at[0])]
    for i in range(DL // TOK):
        place = out_ref.at[pl.ds(TOK, PACK - TOK), pl.ds(i * TOK, TOK)]
        copies.append(
            pltpu.make_async_copy(rot_t_ref.at[pl.ds(16 * i, 16), :], place, sems.at[1 + i])
        )
    for copy in copies:
        copy.start()
    for copy in copies:
        copy.wait()


def pair_kernel(first_ref, second_ref, order_ref, out_ref):
    del order_ref
    out_ref[0:PACK, :] = first_ref[...]
    out_ref[PACK:, :] = second_ref[...]


def head_half(shape, head):
    lane = lax.broadcasted_iota(jnp.int32, shape, 1)
    return (lane >= DR) == (head % 2 == 1)


def rows_kernel(
    lens_ref, shard_ref, q_ref, do_ref, qr_ref, qv_ref, dov_ref, qx_ref, low_ref, qx32_ref, sems
):
    q_copy = pltpu.make_async_copy(q_ref, qv_ref, sems.at[0])
    do_copy = pltpu.make_async_copy(do_ref, dov_ref, sems.at[1])
    q_copy.start()
    do_copy.start()
    for head in range(HEADS):
        pair = qr_ref[:, (head // 2) * 2 * DR : (head // 2 + 1) * 2 * DR].astype(F32)
        qx32_ref[pl.ds(head, TOK, stride=HEADS), :] = jnp.where(
            head_half((TOK, 2 * DR), head), pair, 0.0
        )
    qx_ref[...] = qx32_ref[...].astype(BF16)
    high = lax.broadcasted_iota(jnp.int32, (1, ROWS), 1) // HEADS + FAR
    low = jnp.zeros((1, ROWS), jnp.int32)
    start = (SPAN - shard_ref[0]) * TOK
    for doc in range(lens_ref.shape[0]):
        low = jnp.where(high >= start, start, low)
        start = start + lens_ref[doc]
    low_ref[...] = low
    q_copy.wait()
    do_copy.wait()


def load_keys(ref, slot, keys_ref, rot2_ref):
    rows = slice(slot * TOK, (slot + 1) * TOK)
    keys_ref[rows, :] = ref[0:TOK, :]
    rot_t = load_rotary(ref).astype(F32)
    rot2_ref[rows, :] = jnp.transpose(jnp.concatenate([rot_t, rot_t], axis=0)).astype(BF16)


def near_kernel(
    q_ref, qx_ref, do_ref, own_ref, k2_ref, raw_ref, prob_grad_ref, keys_ref, rot2_ref
):
    load_keys(k2_ref, 0, keys_ref, rot2_ref)
    load_keys(own_ref, 1, keys_ref, rot2_ref)
    raw_ref[...] = dot(keys_ref[...], q_ref[...], NT) + dot(rot2_ref[...], qx_ref[...], NT)
    prob_grad_ref[...] = dot(keys_ref[...], do_ref[...], NT)


def scores_kernel(
    low_ref, q_ref, qx_ref, do_ref, k13_ref, raw_ref, prob_grad_ref, near_ref, near2_ref,
    f13_ref, dst_ref, pt_ref, keys_ref, rot2_ref,
):
    k1_ref = k13_ref.at[pl.ds(0, PACK), :]
    k3_ref = k13_ref.at[pl.ds(PACK, PACK), :]
    load_keys(k3_ref, 0, keys_ref, rot2_ref)
    load_keys(k1_ref, 1, keys_ref, rot2_ref)
    keys_ref[HALF:, :] = near_ref[...]
    rot2_ref[HALF:, :] = near2_ref[...]
    low = low_ref[...]
    high = lax.broadcasted_iota(jnp.int32, (1, ROWS), 1) // HEADS + FAR
    key = lax.broadcasted_iota(jnp.int32, (TOK, CHUNK), 0)
    far = slice(0, HALF)
    for c in range(ROWS // CHUNK):
        cols = slice(c * CHUNK, (c + 1) * CHUNK)
        raw_far = dot(keys_ref[far, :], q_ref[cols, :], NT) + dot(rot2_ref[far, :], qx_ref[cols, :], NT)
        lower = low[:, cols]
        masked = jnp.concatenate(
            [
                jnp.where(key >= lower, raw_far[0:TOK], NEGATIVE),
                jnp.where(key >= lower - 2 * TOK, raw_far[TOK:], NEGATIVE),
                jnp.where(key >= lower - TOK, raw_ref[0:TOK, cols], NEGATIVE),
                jnp.where(
                    (key >= lower - FAR) & (key <= high[:, cols] - FAR), raw_ref[TOK:, cols], NEGATIVE
                ),
            ],
            axis=0,
        )
        peak = jnp.max(masked, axis=0, keepdims=True)
        terms = jnp.exp2((masked - peak) * (SCALE * LOG2_E))
        probs = terms * (1.0 / jnp.sum(terms, axis=0, keepdims=True))
        low_probs = probs.astype(BF16)
        pt_ref[:, cols] = low_probs
        prob_grad = jnp.concatenate(
            [dot(keys_ref[far, :], do_ref[cols, :], NT), prob_grad_ref[:, cols]], axis=0
        )
        delta = jnp.sum(low_probs.astype(F32) * prob_grad, axis=0, keepdims=True)
        dst_ref[:, cols] = (probs * (prob_grad - delta)).astype(BF16)

    grad = SCALE * dot(dst_ref[far, :], q_ref[...], NN) + dot(pt_ref[far, :], do_ref[...], NN)
    rot = SCALE * dot(dst_ref[far, :], qx_ref[...], NN)
    store_tile(f13_ref.at[pl.ds(PACK, PACK), :], grad[0:TOK, :], rot[0:TOK, :])
    store_tile(f13_ref.at[pl.ds(0, PACK), :], grad[TOK:, :], rot[TOK:, :])


def fold_rotary(rot):
    rot_t = jnp.transpose(rot)
    return rot_t[0:DR, :] + rot_t[DR:, :]


def store_tile(ref, grad, rot):
    ref[0:TOK, :] = grad.astype(ref.dtype)
    store_rotary(ref, fold_rotary(rot))


def near_grads_kernel(q_ref, qx_ref, do_ref, dst_ref, pt_ref, f2_ref, g0_ref):
    near = slice(HALF, KEYS)
    grad = SCALE * dot(dst_ref[near, :], q_ref[...], NN) + dot(pt_ref[near, :], do_ref[...], NN)
    rot = SCALE * dot(dst_ref[near, :], qx_ref[...], NN)
    store_tile(f2_ref, grad[0:TOK, :], rot[0:TOK, :])
    store_tile(g0_ref, grad[TOK:, :], rot[TOK:, :])


def queries_kernel(dst_ref, keys_ref, rot2_ref, dq_ref, dqr_ref, x_ref):
    for c in range(ROWS // CHUNK):
        cols = slice(c * CHUNK, (c + 1) * CHUNK)
        ds = jnp.transpose(dst_ref[:, cols])
        dq_ref[cols, :] = (SCALE * dot(ds, keys_ref[...], NN)).astype(BF16)
        x_ref[cols, :] = SCALE * dot(ds, rot2_ref[...], NN)
    for pair in range(HEADS // 2):
        even = x_ref[pl.ds(2 * pair, TOK, stride=HEADS), :]
        odd = x_ref[pl.ds(2 * pair + 1, TOK, stride=HEADS), :]
        dqr_ref[:, pair * 2 * DR : (pair + 1) * 2 * DR] = jnp.where(
            head_half((TOK, 2 * DR), 0), even, odd
        ).astype(BF16)


def relay_kernel(f2_ref, r13_ref, out_ref):
    out_ref[...] = (f2_ref[...] + r13_ref[PACK:, :].astype(F32)).astype(BF16)


def total_kernel(g0_ref, r13_ref, r2_ref, order_ref, out_ref):
    del order_ref
    total = g0_ref[...] + r13_ref[0:PACK, :].astype(F32) + r2_ref[...].astype(F32)
    out_ref[:, 0:DL] = total[0:TOK, :].astype(BF16)
    parts = [total[TOK:, i * TOK : (i + 1) * TOK] for i in range(DL // TOK)]
    rot = jnp.transpose(jnp.concatenate(parts + parts, axis=0))
    out_ref[:, DL:] = rot[:, 0:DR].astype(BF16)


def sum_kernel(blocks_ref, lat_ref, rot_ref):
    total = jnp.sum(blocks_ref[...].astype(F32), axis=0)
    lat_ref[...] = total[:, 0:DL].astype(BF16)
    rot_ref[...] = total[:, DL:].astype(BF16)


def shape(dims, dtype=BF16):
    return jax.ShapeDtypeStruct(dims, dtype)


def call(kernel, outs, spaces, scratch=(), flops=0, moved=0, name=None, limit=24):
    return pl.pallas_call(
        kernel,
        out_shape=outs,
        in_specs=[spec(s) for s in spaces],
        out_specs=jax.tree.map(lambda _: spec(), outs),
        scratch_shapes=scratch,
        compiler_params=pltpu.CompilerParams(vmem_limit_bytes=limit << 20),
        cost_estimate=pl.CostEstimate(flops=flops, bytes_accessed=moved, transcendentals=0),
        name=name,
    )


def in_hbm(x):
    return pltpu.with_memory_space_constraint(x, pltpu.HBM)


def pack(latents, rotary_t):
    return call(
        pack_kernel, shape((PACK, DL)), [HBM] * 2,
        scratch=[pltpu.SemaphoreType.DMA((1 + DL // TOK,))], moved=300000, name="pack",
    )(latents, rotary_t)


def pair_up(first, second, order):
    return call(pair_kernel, shape((2 * PACK, DL)), [VMEM] * 3, moved=600000, name="pair")(
        first, second, order
    )


def row_setup(lens, shard, q, do, qr):
    outs = (shape((ROWS, DL)), shape((ROWS, DL)), shape((ROWS, 2 * DR)), shape((1, ROWS), jnp.int32))
    return call(
        rows_kernel, outs, [SMEM, SMEM, HBM, HBM, VMEM],
        scratch=[pltpu.VMEM((ROWS, 2 * DR), F32), pltpu.SemaphoreType.DMA((2,))],
        moved=4 << 20, name="row_setup",
    )(lens, shard, q, do, qr)


def near_scores(q, qx, do, own, k2):
    outs = (
        shape((HALF, ROWS), F32), shape((HALF, ROWS), F32), shape((HALF, DL)), shape((HALF, 2 * DR)),
    )
    return call(
        near_kernel, outs, [VMEM] * 5, flops=2 * ROWS * KEYS * DL, moved=4 << 20, name="near_scores"
    )(q, qx, do, own, k2)


def scores(low, q, qx, do, k13, raw, prob_grad, near, near2):
    outs = (
        shape((2 * PACK, DL)), shape((KEYS, ROWS)), shape((KEYS, ROWS)),
        shape((KEYS, DL)), shape((KEYS, 2 * DR)),
    )
    return call(
        scores_kernel, outs, [VMEM] * 9,
        flops=2 * ROWS * KEYS * DL * 2, moved=6 << 20, name="scores",
    )(low, q, qx, do, k13, raw, prob_grad, near, near2)


def near_grads(q, qx, do, dst, pt):
    tile = shape((PACK, DL), F32)
    return call(
        near_grads_kernel, (tile, tile), [VMEM] * 5,
        flops=2 * ROWS * KEYS * DL, moved=4 << 20, name="near_grads",
    )(q, qx, do, dst, pt)


def queries(dst, keys, rot2):
    outs = (shape((ROWS, DL)), shape((TOK, HEADS * DR)))
    return call(
        queries_kernel, outs, [VMEM] * 3, scratch=[pltpu.VMEM((ROWS, 2 * DR), F32)],
        flops=2 * ROWS * KEYS * DL, moved=4 << 20, name="queries",
    )(dst, keys, rot2)


def relay(f2, r13):
    return call(relay_kernel, shape((PACK, DL)), [VMEM] * 2, moved=600000, name="relay")(f2, r13)


def total(g0, r13, r2, order):
    return call(
        total_kernel, shape((TOK, DL + DR)), [VMEM] * 3 + [HBM], moved=1 << 20, name="total"
    )(g0, r13, r2, order)


def head_sum(blocks):
    rows = blocks.shape[1]
    return call(
        sum_kernel, (shape((rows, DL)), shape((rows, DR))), [VMEM], moved=200000, name="head_sum"
    )(blocks)


def shifted(block, axis, distance):
    devices = range(lax.axis_size(axis))
    route = [(i - distance, i) for i in devices if i - distance in devices]
    return lax.ppermute(block, axis, route)


def body(query_latent, query_rotary, latents, key_rotary, out_grad, doc_lengths):
    head_devices = lax.axis_size("head")
    shard = jnp.reshape(lax.axis_index("tok"), (1,)).astype(jnp.int32)
    q = query_latent.reshape(ROWS, DL)
    do = out_grad.reshape(ROWS, DL)
    own = pack(in_hbm(latents), in_hbm(key_rotary.T))
    k2 = shifted(own, "tok", 2)
    q, do, qx, low = row_setup(doc_lengths, shard, in_hbm(q), in_hbm(do), query_rotary)
    k13 = shifted(pair_up(own, k2, low), "tok", 1)
    raw, prob_grad, near, near2 = near_scores(q, qx, do, own, k2)
    f13, dst, pt, keys, rot2 = scores(low, q, qx, do, k13, raw, prob_grad, near, near2)
    r13 = shifted(f13, "tok", -1)
    f2, g0 = near_grads(q, qx, do, dst, pt)
    r2 = shifted(relay(f2, r13), "tok", -2)
    dq, dqr = queries(dst, keys, rot2)
    blocks = total(g0, r13, r2, in_hbm(dqr)).reshape(head_devices, TOK // head_devices, DL + DR)
    blocks = lax.all_to_all(blocks, "head", split_axis=0, concat_axis=0, tiled=True)
    grad_latents, grad_key_rotary = head_sum(blocks)
    return dq.reshape(TOK, HEADS, DL), dqr, grad_latents, grad_key_rotary


def solution(mesh):
    in_specs = (
        P("tok", "head", None),
        P("tok", "head"),
        P("tok", None),
        P("tok", None),
        P("tok", "head", None),
        P(),
    )
    out_specs = (
        P("tok", "head", None),
        P("tok", "head"),
        P(("tok", "head"), None),
        P(("tok", "head"), None),
    )
    return jax.shard_map(body, mesh=mesh, in_specs=in_specs, out_specs=out_specs, check_vma=False)
```

```python
import jax
import jax.numpy as jnp
from jax import lax
from jax.experimental import pallas as pl
from jax.experimental.pallas import tpu as pltpu
from jax.sharding import PartitionSpec as P

SPAN = 3


SCALE = 0.07216878364870322
LOG2_E = 1.4426950408889634
NEGATIVE = -1e30

TOK = 128
HEADS = 8
DL = 512
DR = 64
ROWS = TOK * HEADS
KEYS = (SPAN + 1) * TOK
FAR = SPAN * TOK
PACK = TOK + TOK * DR // DL
CHUNK = 256
HALF = KEYS // 2

F32 = jnp.float32
BF16 = jnp.bfloat16
VMEM = pltpu.MemorySpace.VMEM
SMEM = pltpu.MemorySpace.SMEM
HBM = pltpu.MemorySpace.HBM

NT = (((1,), (1,)), ((), ()))
NN = (((1,), (0,)), ((), ()))


def dot(a, b, dims):
    return lax.dot_general(a, b, dims, preferred_element_type=F32)


def spec(space=VMEM):
    return pl.BlockSpec(memory_space=space)


def store_rotary(ref, rotary_t):
    for i in range(DL // TOK):
        ref[TOK:PACK, i * TOK : (i + 1) * TOK] = rotary_t[16 * i : 16 * (i + 1), :].astype(ref.dtype)


def load_rotary(ref):
    parts = [ref[TOK:PACK, i * TOK : (i + 1) * TOK] for i in range(DL // TOK)]
    return jnp.concatenate(parts, axis=0)


def pack_kernel(lat_ref, rot_t_ref, out_ref, sems):
    copies = [pltpu.make_async_copy(lat_ref, out_ref.at[pl.ds(0, TOK), :], sems.at[0])]
    for i in range(DL // TOK):
        place = out_ref.at[pl.ds(TOK, PACK - TOK), pl.ds(i * TOK, TOK)]
        copies.append(
            pltpu.make_async_copy(rot_t_ref.at[pl.ds(16 * i, 16), :], place, sems.at[1 + i])
        )
    for copy in copies:
        copy.start()
    for copy in copies:
        copy.wait()


def head_half(shape, head):
    lane = lax.broadcasted_iota(jnp.int32, shape, 1)
    return (lane >= DR) == (head % 2 == 1)


def rows_kernel(
    lens_ref, shard_ref, q_ref, do_ref, qr_ref, qv_ref, dov_ref, qx_ref, low_ref, qx32_ref, sems
):
    q_copy = pltpu.make_async_copy(q_ref, qv_ref, sems.at[0])
    do_copy = pltpu.make_async_copy(do_ref, dov_ref, sems.at[1])
    q_copy.start()
    do_copy.start()
    for head in range(HEADS):
        pair = qr_ref[:, (head // 2) * 2 * DR : (head // 2 + 1) * 2 * DR].astype(F32)
        qx32_ref[pl.ds(head, TOK, stride=HEADS), :] = jnp.where(
            head_half((TOK, 2 * DR), head), pair, 0.0
        )
    qx_ref[...] = qx32_ref[...].astype(BF16)
    high = lax.broadcasted_iota(jnp.int32, (1, ROWS), 1) // HEADS + FAR
    low = jnp.zeros((1, ROWS), jnp.int32)
    start = (SPAN - shard_ref[0]) * TOK
    for doc in range(lens_ref.shape[0]):
        low = jnp.where(high >= start, start, low)
        start = start + lens_ref[doc]
    low_ref[...] = low
    q_copy.wait()
    do_copy.wait()


def load_keys(ref, slot, keys_ref, rot2_ref):
    rows = slice(slot * TOK, (slot + 1) * TOK)
    keys_ref[rows, :] = ref[0:TOK, :]
    rot_t = load_rotary(ref).astype(F32)
    rot2_ref[rows, :] = jnp.transpose(jnp.concatenate([rot_t, rot_t], axis=0)).astype(BF16)


def near_kernel(
    q_ref, qx_ref, do_ref, own_ref, k2_ref, raw_ref, prob_grad_ref, keys_ref, rot2_ref
):
    load_keys(k2_ref, 0, keys_ref, rot2_ref)
    load_keys(own_ref, 1, keys_ref, rot2_ref)
    raw_ref[...] = dot(keys_ref[...], q_ref[...], NT) + dot(rot2_ref[...], qx_ref[...], NT)
    prob_grad_ref[...] = dot(keys_ref[...], do_ref[...], NT)


def scores_kernel(
    low_ref, q_ref, qx_ref, do_ref, k1_ref, k3_ref, raw_ref, prob_grad_ref, near_ref, near2_ref,
    f3_ref, f2_ref, f1_ref, dst_ref, pt_ref, keys_ref, rot2_ref,
):
    load_keys(k3_ref, 0, keys_ref, rot2_ref)
    load_keys(k1_ref, 1, keys_ref, rot2_ref)
    keys_ref[HALF:, :] = near_ref[...]
    rot2_ref[HALF:, :] = near2_ref[...]
    low = low_ref[...]
    high = lax.broadcasted_iota(jnp.int32, (1, ROWS), 1) // HEADS + FAR
    key = lax.broadcasted_iota(jnp.int32, (TOK, CHUNK), 0)
    far = slice(0, HALF)
    for c in range(ROWS // CHUNK):
        cols = slice(c * CHUNK, (c + 1) * CHUNK)
        raw_far = dot(keys_ref[far, :], q_ref[cols, :], NT) + dot(rot2_ref[far, :], qx_ref[cols, :], NT)
        lower = low[:, cols]
        masked = jnp.concatenate(
            [
                jnp.where(key >= lower, raw_far[0:TOK], NEGATIVE),
                jnp.where(key >= lower - 2 * TOK, raw_far[TOK:], NEGATIVE),
                jnp.where(key >= lower - TOK, raw_ref[0:TOK, cols], NEGATIVE),
                jnp.where(
                    (key >= lower - FAR) & (key <= high[:, cols] - FAR), raw_ref[TOK:, cols], NEGATIVE
                ),
            ],
            axis=0,
        )
        peak = jnp.max(masked, axis=0, keepdims=True)
        terms = jnp.exp2((masked - peak) * (SCALE * LOG2_E))
        probs = terms * (1.0 / jnp.sum(terms, axis=0, keepdims=True))
        low_probs = probs.astype(BF16)
        pt_ref[:, cols] = low_probs
        prob_grad = jnp.concatenate(
            [dot(keys_ref[far, :], do_ref[cols, :], NT), prob_grad_ref[:, cols]], axis=0
        )
        delta = jnp.sum(low_probs.astype(F32) * prob_grad, axis=0, keepdims=True)
        dst_ref[:, cols] = (probs * (prob_grad - delta)).astype(BF16)

    earlier = slice(0, FAR)
    grad = SCALE * dot(dst_ref[earlier, :], q_ref[...], NN) + dot(pt_ref[earlier, :], do_ref[...], NN)
    rot = SCALE * dot(dst_ref[earlier, :], qx_ref[...], NN)
    for slot, ref in enumerate((f3_ref, f1_ref, f2_ref)):
        rows = slice(slot * TOK, (slot + 1) * TOK)
        store_tile(ref, grad[rows, :], rot[rows, :])


def fold_rotary(rot):
    rot_t = jnp.transpose(rot)
    return rot_t[0:DR, :] + rot_t[DR:, :]


def store_tile(ref, grad, rot):
    ref[0:TOK, :] = grad.astype(ref.dtype)
    store_rotary(ref, fold_rotary(rot))


def queries_kernel(
    q_ref, qx_ref, do_ref, dst_ref, pt_ref, keys_ref, rot2_ref, dq_ref, dqr_ref, g0_ref, x_ref
):
    own = slice(FAR, KEYS)
    grad = SCALE * dot(dst_ref[own, :], q_ref[...], NN) + dot(pt_ref[own, :], do_ref[...], NN)
    store_tile(g0_ref, grad, SCALE * dot(dst_ref[own, :], qx_ref[...], NN))
    for c in range(ROWS // CHUNK):
        cols = slice(c * CHUNK, (c + 1) * CHUNK)
        ds = jnp.transpose(dst_ref[:, cols])
        dq_ref[cols, :] = (SCALE * dot(ds, keys_ref[...], NN)).astype(BF16)
        x_ref[cols, :] = SCALE * dot(ds, rot2_ref[...], NN)
    for pair in range(HEADS // 2):
        even = x_ref[pl.ds(2 * pair, TOK, stride=HEADS), :]
        odd = x_ref[pl.ds(2 * pair + 1, TOK, stride=HEADS), :]
        dqr_ref[:, pair * 2 * DR : (pair + 1) * 2 * DR] = jnp.where(
            head_half((TOK, 2 * DR), 0), even, odd
        ).astype(BF16)


def total_kernel(g0_ref, r1_ref, r2_ref, r3_ref, out_ref):
    total = g0_ref[...]
    for ref in (r1_ref, r2_ref, r3_ref):
        total = total + ref[...].astype(F32)
    out_ref[:, 0:DL] = total[0:TOK, :].astype(BF16)
    parts = [total[TOK:, i * TOK : (i + 1) * TOK] for i in range(DL // TOK)]
    rot = jnp.transpose(jnp.concatenate(parts + parts, axis=0))
    out_ref[:, DL:] = rot[:, 0:DR].astype(BF16)


def sum_kernel(blocks_ref, lat_ref, rot_ref):
    total = jnp.sum(blocks_ref[...].astype(F32), axis=0)
    lat_ref[...] = total[:, 0:DL].astype(BF16)
    rot_ref[...] = total[:, DL:].astype(BF16)


def shape(dims, dtype=BF16):
    return jax.ShapeDtypeStruct(dims, dtype)


def call(kernel, outs, spaces, scratch=(), flops=0, moved=0, name=None, limit=24):
    return pl.pallas_call(
        kernel,
        out_shape=outs,
        in_specs=[spec(s) for s in spaces],
        out_specs=jax.tree.map(lambda _: spec(), outs),
        scratch_shapes=scratch,
        compiler_params=pltpu.CompilerParams(vmem_limit_bytes=limit << 20),
        cost_estimate=pl.CostEstimate(flops=flops, bytes_accessed=moved, transcendentals=0),
        name=name,
    )


def in_hbm(x):
    return pltpu.with_memory_space_constraint(x, pltpu.HBM)


def pack(latents, rotary_t):
    return call(
        pack_kernel, shape((PACK, DL)), [HBM] * 2,
        scratch=[pltpu.SemaphoreType.DMA((1 + DL // TOK,))], moved=300000, name="pack",
    )(latents, rotary_t)


def row_setup(lens, shard, q, do, qr):
    outs = (shape((ROWS, DL)), shape((ROWS, DL)), shape((ROWS, 2 * DR)), shape((1, ROWS), jnp.int32))
    return call(
        rows_kernel, outs, [SMEM, SMEM, HBM, HBM, VMEM],
        scratch=[pltpu.VMEM((ROWS, 2 * DR), F32), pltpu.SemaphoreType.DMA((2,))],
        moved=4 << 20, name="row_setup",
    )(lens, shard, q, do, qr)


def near_scores(q, qx, do, own, k2):
    outs = (
        shape((HALF, ROWS), F32), shape((HALF, ROWS), F32), shape((HALF, DL)), shape((HALF, 2 * DR)),
    )
    return call(
        near_kernel, outs, [VMEM] * 5, flops=2 * ROWS * KEYS * DL, moved=4 << 20, name="near_scores"
    )(q, qx, do, own, k2)


def scores(low, q, qx, do, k1, k3, raw, prob_grad, near, near2):
    tile = shape((PACK, DL))
    outs = (
        tile, tile, tile, shape((KEYS, ROWS)), shape((KEYS, ROWS)),
        shape((KEYS, DL)), shape((KEYS, 2 * DR)),
    )
    return call(
        scores_kernel, outs, [VMEM] * 10,
        flops=2 * ROWS * KEYS * DL * 2, moved=6 << 20, name="scores",
    )(low, q, qx, do, k1, k3, raw, prob_grad, near, near2)


def queries(q, qx, do, dst, pt, keys, rot2):
    outs = (shape((ROWS, DL)), shape((TOK, HEADS * DR)), shape((PACK, DL), F32))
    return call(
        queries_kernel, outs, [VMEM] * 7, scratch=[pltpu.VMEM((ROWS, 2 * DR), F32)],
        flops=2 * ROWS * KEYS * DL * 2, moved=6 << 20, name="queries",
    )(q, qx, do, dst, pt, keys, rot2)


def total(g0, r1, r2, r3):
    return call(
        total_kernel, shape((TOK, DL + DR)), [VMEM] * 4, moved=1 << 20, name="total"
    )(g0, r1, r2, r3)


def head_sum(blocks):
    rows = blocks.shape[1]
    return call(
        sum_kernel, (shape((rows, DL)), shape((rows, DR))), [VMEM], moved=200000, name="head_sum"
    )(blocks)


def shifted(block, axis, distance):
    devices = range(lax.axis_size(axis))
    route = [(i - distance, i) for i in devices if i - distance in devices]
    return lax.ppermute(block, axis, route)


def body(query_latent, query_rotary, latents, key_rotary, out_grad, doc_lengths):
    head_devices = lax.axis_size("head")
    shard = jnp.reshape(lax.axis_index("tok"), (1,)).astype(jnp.int32)
    q = query_latent.reshape(ROWS, DL)
    do = out_grad.reshape(ROWS, DL)
    own = pack(in_hbm(latents), in_hbm(key_rotary.T))
    k1, k3, k2 = [shifted(own, "tok", distance) for distance in (1, 3, 2)]
    q, do, qx, low = row_setup(doc_lengths, shard, in_hbm(q), in_hbm(do), query_rotary)
    raw, prob_grad, near, near2 = near_scores(q, qx, do, own, k2)
    f3, f2, f1, dst, pt, keys, rot2 = scores(low, q, qx, do, k1, k3, raw, prob_grad, near, near2)
    r1, r2, r3 = [shifted(f, "tok", -d) for d, f in ((1, f1), (2, f2), (3, f3))]
    dq, dqr, g0 = queries(q, qx, do, dst, pt, keys, rot2)
    blocks = total(g0, r1, r2, r3).reshape(head_devices, TOK // head_devices, DL + DR)
    blocks = lax.all_to_all(blocks, "head", split_axis=0, concat_axis=0, tiled=True)
    grad_latents, grad_key_rotary = head_sum(blocks)
    return dq.reshape(TOK, HEADS, DL), dqr, grad_latents, grad_key_rotary


def solution(mesh):
    in_specs = (
        P("tok", "head", None),
        P("tok", "head"),
        P("tok", None),
        P("tok", None),
        P("tok", "head", None),
        P(),
    )
    out_specs = (
        P("tok", "head", None),
        P("tok", "head"),
        P(("tok", "head"), None),
        P(("tok", "head"), None),
    )
    return jax.shard_map(body, mesh=mesh, in_specs=in_specs, out_specs=out_specs, check_vma=False)
```

```python
import jax
import jax.numpy as jnp
from jax import lax
from jax.experimental import pallas as pl
from jax.experimental.pallas import tpu as pltpu
from jax.sharding import PartitionSpec as P

SPAN = 3


SCALE = 0.07216878364870322
LOG2_E = 1.4426950408889634
NEGATIVE = -1e30

TOK = 128
HEADS = 8
DL = 512
DR = 64
ROWS = TOK * HEADS
KEYS = (SPAN + 1) * TOK
FAR = SPAN * TOK
PACK = TOK + TOK * DR // DL
CHUNK = 256
HALF = KEYS // 2
FETCHES = 4

F32 = jnp.float32
BF16 = jnp.bfloat16
VMEM = pltpu.MemorySpace.VMEM
SMEM = pltpu.MemorySpace.SMEM
HBM = pltpu.MemorySpace.HBM

NT = (((1,), (1,)), ((), ()))
NN = (((1,), (0,)), ((), ()))


def dot(a, b, dims):
    return lax.dot_general(a, b, dims, preferred_element_type=F32)


def spec(space=VMEM):
    return pl.BlockSpec(memory_space=space)


def store_rotary(ref, rotary_t):
    for i in range(DL // TOK):
        ref[TOK:PACK, i * TOK : (i + 1) * TOK] = rotary_t[16 * i : 16 * (i + 1), :].astype(ref.dtype)


def load_rotary(ref):
    parts = [ref[TOK:PACK, i * TOK : (i + 1) * TOK] for i in range(DL // TOK)]
    return jnp.concatenate(parts, axis=0)


def pack_kernel(lat_ref, rot_t_ref, out_ref, sems):
    copies = [pltpu.make_async_copy(lat_ref, out_ref.at[pl.ds(0, TOK), :], sems.at[0])]
    for i in range(DL // TOK):
        place = out_ref.at[pl.ds(TOK, PACK - TOK), pl.ds(i * TOK, TOK)]
        copies.append(
            pltpu.make_async_copy(rot_t_ref.at[pl.ds(16 * i, 16), :], place, sems.at[1 + i])
        )
    for copy in copies:
        copy.start()
    for copy in copies:
        copy.wait()


def head_half(shape, head):
    lane = lax.broadcasted_iota(jnp.int32, shape, 1)
    return (lane >= DR) == (head % 2 == 1)


def shard_index():
    return lax.axis_index("tok").astype(jnp.int32)


def rows_kernel(
    lens_ref, q_ref, do_ref, qr_ref, qv_ref, dov_ref, qx_ref, low_ref, lens_smem, qx32_ref, sems
):
    copies = []
    for i in range(FETCHES):
        part = pl.ds(i * ROWS // FETCHES, ROWS // FETCHES)
        copies.append(pltpu.make_async_copy(q_ref.at[part, :], qv_ref.at[part, :], sems.at[2 * i]))
        copies.append(
            pltpu.make_async_copy(do_ref.at[part, :], dov_ref.at[part, :], sems.at[2 * i + 1])
        )
    lens_copy = pltpu.make_async_copy(lens_ref, lens_smem, sems.at[2 * FETCHES])
    lens_copy.start()
    for copy in copies:
        copy.start()
    for head in range(HEADS):
        pair = qr_ref[:, (head // 2) * 2 * DR : (head // 2 + 1) * 2 * DR].astype(F32)
        qx32_ref[pl.ds(head, TOK, stride=HEADS), :] = jnp.where(
            head_half((TOK, 2 * DR), head), pair, 0.0
        )
    qx_ref[...] = qx32_ref[...].astype(BF16)
    high = lax.broadcasted_iota(jnp.int32, (1, ROWS), 1) // HEADS + FAR
    low = jnp.zeros((1, ROWS), jnp.int32)
    start = (SPAN - shard_index()) * TOK
    lens_copy.wait()
    for doc in range(lens_smem.shape[0]):
        low = jnp.where(high >= start, start, low)
        start = start + lens_smem[doc]
    low_ref[...] = low
    for copy in copies:
        copy.wait()


def load_keys(ref, slot, keys_ref, rot2_ref):
    rows = slice(slot * TOK, (slot + 1) * TOK)
    keys_ref[rows, :] = ref[0:TOK, :]
    rot_t = load_rotary(ref).astype(F32)
    rot2_ref[rows, :] = jnp.transpose(jnp.concatenate([rot_t, rot_t], axis=0)).astype(BF16)


def near_kernel(
    q_ref, qx_ref, do_ref, own_ref, k2_ref, raw_ref, prob_grad_ref, keys_ref, rot2_ref
):
    load_keys(k2_ref, 0, keys_ref, rot2_ref)
    load_keys(own_ref, 1, keys_ref, rot2_ref)
    raw_ref[...] = dot(keys_ref[...], q_ref[...], NT) + dot(rot2_ref[...], qx_ref[...], NT)
    prob_grad_ref[...] = dot(keys_ref[...], do_ref[...], NT)


def scores_kernel(
    low_ref, q_ref, qx_ref, do_ref, k1_ref, k3_ref, raw_ref, prob_grad_ref, near_ref, near2_ref,
    f3_ref, f2_ref, f1_ref, dst_ref, pt_ref, keys_ref, rot2_ref,
):
    load_keys(k3_ref, 0, keys_ref, rot2_ref)
    load_keys(k1_ref, 1, keys_ref, rot2_ref)
    keys_ref[HALF:, :] = near_ref[...]
    rot2_ref[HALF:, :] = near2_ref[...]
    low = low_ref[...]
    high = lax.broadcasted_iota(jnp.int32, (1, ROWS), 1) // HEADS + FAR
    key = lax.broadcasted_iota(jnp.int32, (TOK, CHUNK), 0)
    far = slice(0, HALF)
    for c in range(ROWS // CHUNK):
        cols = slice(c * CHUNK, (c + 1) * CHUNK)
        raw_far = dot(keys_ref[far, :], q_ref[cols, :], NT) + dot(rot2_ref[far, :], qx_ref[cols, :], NT)
        lower = low[:, cols]
        masked = jnp.concatenate(
            [
                jnp.where(key >= lower, raw_far[0:TOK], NEGATIVE),
                jnp.where(key >= lower - 2 * TOK, raw_far[TOK:], NEGATIVE),
                jnp.where(key >= lower - TOK, raw_ref[0:TOK, cols], NEGATIVE),
                jnp.where(
                    (key >= lower - FAR) & (key <= high[:, cols] - FAR), raw_ref[TOK:, cols], NEGATIVE
                ),
            ],
            axis=0,
        )
        peak = jnp.max(masked, axis=0, keepdims=True)
        terms = jnp.exp2((masked - peak) * (SCALE * LOG2_E))
        probs = terms * (1.0 / jnp.sum(terms, axis=0, keepdims=True))
        low_probs = probs.astype(BF16)
        pt_ref[:, cols] = low_probs
        prob_grad = jnp.concatenate(
            [dot(keys_ref[far, :], do_ref[cols, :], NT), prob_grad_ref[:, cols]], axis=0
        )
        delta = jnp.sum(low_probs.astype(F32) * prob_grad, axis=0, keepdims=True)
        dst_ref[:, cols] = (probs * (prob_grad - delta)).astype(BF16)

    earlier = slice(0, FAR)
    grad = SCALE * dot(dst_ref[earlier, :], q_ref[...], NN) + dot(pt_ref[earlier, :], do_ref[...], NN)
    rot = SCALE * dot(dst_ref[earlier, :], qx_ref[...], NN)
    for slot, ref in enumerate((f3_ref, f1_ref, f2_ref)):
        rows = slice(slot * TOK, (slot + 1) * TOK)
        store_tile(ref, grad[rows, :], rot[rows, :])


def fold_rotary(rot):
    rot_t = jnp.transpose(rot)
    return rot_t[0:DR, :] + rot_t[DR:, :]


def store_tile(ref, grad, rot):
    ref[0:TOK, :] = grad.astype(ref.dtype)
    store_rotary(ref, fold_rotary(rot))


def queries_kernel(
    q_ref, qx_ref, do_ref, dst_ref, pt_ref, keys_ref, rot2_ref, dq_ref, dqr_ref, g0_ref, x_ref
):
    own = slice(FAR, KEYS)
    grad = SCALE * dot(dst_ref[own, :], q_ref[...], NN) + dot(pt_ref[own, :], do_ref[...], NN)
    store_tile(g0_ref, grad, SCALE * dot(dst_ref[own, :], qx_ref[...], NN))
    for c in range(ROWS // CHUNK):
        cols = slice(c * CHUNK, (c + 1) * CHUNK)
        ds = jnp.transpose(dst_ref[:, cols])
        dq_ref[cols, :] = (SCALE * dot(ds, keys_ref[...], NN)).astype(BF16)
        x_ref[cols, :] = SCALE * dot(ds, rot2_ref[...], NN)
    for pair in range(HEADS // 2):
        even = x_ref[pl.ds(2 * pair, TOK, stride=HEADS), :]
        odd = x_ref[pl.ds(2 * pair + 1, TOK, stride=HEADS), :]
        dqr_ref[:, pair * 2 * DR : (pair + 1) * 2 * DR] = jnp.where(
            head_half((TOK, 2 * DR), 0), even, odd
        ).astype(BF16)


def total_kernel(g0_ref, r3_ref, r2_ref, r1_ref, out_ref):
    total = g0_ref[...]
    for ref in (r3_ref, r2_ref, r1_ref):
        total = total + ref[...].astype(F32)
    out_ref[:, 0:DL] = total[0:TOK, :].astype(BF16)
    parts = [total[TOK:, i * TOK : (i + 1) * TOK] for i in range(DL // TOK)]
    rot = jnp.transpose(jnp.concatenate(parts + parts, axis=0))
    out_ref[:, DL:] = rot[:, 0:DR].astype(BF16)


def sum_kernel(blocks_ref, lat_ref, rot_ref):
    total = jnp.sum(blocks_ref[...].astype(F32), axis=0)
    lat_ref[...] = total[:, 0:DL].astype(BF16)
    rot_ref[...] = total[:, DL:].astype(BF16)


def shape(dims, dtype=BF16):
    return jax.ShapeDtypeStruct(dims, dtype)


def call(kernel, outs, spaces, scratch=(), flops=0, moved=0, name=None, limit=24):
    return pl.pallas_call(
        kernel,
        out_shape=outs,
        in_specs=[spec(s) for s in spaces],
        out_specs=jax.tree.map(lambda _: spec(), outs),
        scratch_shapes=scratch,
        compiler_params=pltpu.CompilerParams(vmem_limit_bytes=limit << 20),
        cost_estimate=pl.CostEstimate(flops=flops, bytes_accessed=moved, transcendentals=0),
        name=name,
    )


def in_hbm(x):
    return pltpu.with_memory_space_constraint(x, pltpu.HBM)


def pack(latents, rotary_t):
    return call(
        pack_kernel, shape((PACK, DL)), [HBM] * 2,
        scratch=[pltpu.SemaphoreType.DMA((1 + DL // TOK,))], moved=300000, name="pack",
    )(latents, rotary_t)


def row_setup(lens, q, do, qr):
    outs = (shape((ROWS, DL)), shape((ROWS, DL)), shape((ROWS, 2 * DR)), shape((1, ROWS), jnp.int32))
    return call(
        rows_kernel, outs, [HBM, HBM, HBM, VMEM],
        scratch=[
            pltpu.SMEM(lens.shape, jnp.int32),
            pltpu.VMEM((ROWS, 2 * DR), F32),
            pltpu.SemaphoreType.DMA((2 * FETCHES + 1,)),
        ],
        moved=4 << 20, name="row_setup",
    )(lens, q, do, qr)


def near_scores(q, qx, do, own, k2):
    outs = (
        shape((HALF, ROWS), F32), shape((HALF, ROWS), F32), shape((HALF, DL)), shape((HALF, 2 * DR)),
    )
    return call(
        near_kernel, outs, [VMEM] * 5, flops=2 * ROWS * KEYS * DL, moved=4 << 20, name="near_scores"
    )(q, qx, do, own, k2)


def scores(low, q, qx, do, k1, k3, raw, prob_grad, near, near2):
    tile = shape((PACK, DL))
    outs = (
        tile, tile, tile, shape((KEYS, ROWS)), shape((KEYS, ROWS)),
        shape((KEYS, DL)), shape((KEYS, 2 * DR)),
    )
    return call(
        scores_kernel, outs, [VMEM] * 10,
        flops=2 * ROWS * KEYS * DL * 2, moved=6 << 20, name="scores",
    )(low, q, qx, do, k1, k3, raw, prob_grad, near, near2)


def queries(q, qx, do, dst, pt, keys, rot2):
    outs = (shape((ROWS, DL)), shape((TOK, HEADS * DR)), shape((PACK, DL), F32))
    return call(
        queries_kernel, outs, [VMEM] * 7, scratch=[pltpu.VMEM((ROWS, 2 * DR), F32)],
        flops=2 * ROWS * KEYS * DL * 2, moved=6 << 20, name="queries",
    )(q, qx, do, dst, pt, keys, rot2)


def total(g0, r3, r2, r1):
    return call(
        total_kernel, shape((TOK, DL + DR)), [VMEM] * 4, moved=1 << 20, name="total"
    )(g0, r3, r2, r1)


def head_sum(blocks):
    rows = blocks.shape[1]
    return call(
        sum_kernel, (shape((rows, DL)), shape((rows, DR))), [VMEM], moved=200000, name="head_sum"
    )(blocks)


def shifted(block, axis, distance):
    devices = range(lax.axis_size(axis))
    route = [(i - distance, i) for i in devices if i - distance in devices]
    return lax.ppermute(block, axis, route)


def body(query_latent, query_rotary, latents, key_rotary, out_grad, doc_lengths):
    head_devices = lax.axis_size("head")
    q = query_latent.reshape(ROWS, DL)
    do = out_grad.reshape(ROWS, DL)
    own = pack(in_hbm(latents), in_hbm(key_rotary.T))
    k1, k3, k2 = [shifted(own, "tok", distance) for distance in (1, 3, 2)]
    q, do, qx, low = row_setup(in_hbm(doc_lengths), in_hbm(q), in_hbm(do), query_rotary)
    raw, prob_grad, near, near2 = near_scores(q, qx, do, own, k2)
    f3, f2, f1, dst, pt, keys, rot2 = scores(low, q, qx, do, k1, k3, raw, prob_grad, near, near2)
    r3, r2, r1 = [shifted(f, "tok", -d) for d, f in ((3, f3), (2, f2), (1, f1))]
    dq, dqr, g0 = queries(q, qx, do, dst, pt, keys, rot2)
    blocks = total(g0, r3, r2, r1).reshape(head_devices, TOK // head_devices, DL + DR)
    blocks = lax.all_to_all(blocks, "head", split_axis=0, concat_axis=0, tiled=True)
    grad_latents, grad_key_rotary = head_sum(blocks)
    return dq.reshape(TOK, HEADS, DL), dqr, grad_latents, grad_key_rotary


def solution(mesh):
    in_specs = (
        P("tok", "head", None),
        P("tok", "head"),
        P("tok", None),
        P("tok", None),
        P("tok", "head", None),
        P(),
    )
    out_specs = (
        P("tok", "head", None),
        P("tok", "head"),
        P(("tok", "head"), None),
        P(("tok", "head"), None),
    )
    return jax.shard_map(body, mesh=mesh, in_specs=in_specs, out_specs=out_specs, check_vma=False)
```

```python
import jax
import jax.numpy as jnp
from jax import lax
from jax.experimental import pallas as pl
from jax.experimental.pallas import tpu as pltpu
from jax.sharding import PartitionSpec as P

SPAN = 3


SCALE = 0.07216878364870322
LOG2_E = 1.4426950408889634
NEGATIVE = -1e30

TOK = 128
HEADS = 8
DL = 512
DR = 64
ROWS = TOK * HEADS
KEYS = (SPAN + 1) * TOK
FAR = SPAN * TOK
PACK = TOK + TOK * DR // DL
CHUNK = 256
HALF = KEYS // 2
BLOCK = 2 * (DL // TOK) + 1
FETCHES = 4

F32 = jnp.float32
BF16 = jnp.bfloat16
VMEM = pltpu.MemorySpace.VMEM
SMEM = pltpu.MemorySpace.SMEM
HBM = pltpu.MemorySpace.HBM

NT = (((1,), (1,)), ((), ()))
NN = (((1,), (0,)), ((), ()))


def dot(a, b, dims):
    return lax.dot_general(a, b, dims, preferred_element_type=F32)


def spec(space=VMEM):
    return pl.BlockSpec(memory_space=space)


def store_rotary(ref, rotary_t):
    for i in range(DL // TOK):
        ref[TOK:PACK, i * TOK : (i + 1) * TOK] = rotary_t[16 * i : 16 * (i + 1), :].astype(ref.dtype)


def load_rotary(ref):
    parts = [ref[TOK:PACK, i * TOK : (i + 1) * TOK] for i in range(DL // TOK)]
    return jnp.concatenate(parts, axis=0)


def pack_kernel(lat_ref, rot_t_ref, out_ref, sems):
    copies = [pltpu.make_async_copy(lat_ref, out_ref.at[pl.ds(0, TOK), :], sems.at[0])]
    for i in range(DL // TOK):
        place = out_ref.at[pl.ds(TOK, PACK - TOK), pl.ds(i * TOK, TOK)]
        copies.append(
            pltpu.make_async_copy(rot_t_ref.at[pl.ds(16 * i, 16), :], place, sems.at[1 + i])
        )
    for copy in copies:
        copy.start()
    for copy in copies:
        copy.wait()


def head_half(shape, head):
    lane = lax.broadcasted_iota(jnp.int32, shape, 1)
    return (lane >= DR) == (head % 2 == 1)


def shard_index():
    return lax.axis_index("tok").astype(jnp.int32)


def rows_kernel(
    lens_ref, q_ref, do_ref, qr_ref, qv_ref, dov_ref, qx_ref, low_ref, lens_smem, qx32_ref, sems
):
    copies = []
    for i in range(FETCHES):
        part = pl.ds(i * ROWS // FETCHES, ROWS // FETCHES)
        copies.append(pltpu.make_async_copy(q_ref.at[part, :], qv_ref.at[part, :], sems.at[2 * i]))
        copies.append(
            pltpu.make_async_copy(do_ref.at[part, :], dov_ref.at[part, :], sems.at[2 * i + 1])
        )
    lens_copy = pltpu.make_async_copy(lens_ref, lens_smem, sems.at[2 * FETCHES])
    lens_copy.start()
    for copy in copies:
        copy.start()
    for head in range(HEADS):
        pair = qr_ref[:, (head // 2) * 2 * DR : (head // 2 + 1) * 2 * DR].astype(F32)
        qx32_ref[pl.ds(head, TOK, stride=HEADS), :] = jnp.where(
            head_half((TOK, 2 * DR), head), pair, 0.0
        )
    qx_ref[...] = qx32_ref[...].astype(BF16)
    high = lax.broadcasted_iota(jnp.int32, (1, ROWS), 1) // HEADS + FAR
    low = jnp.zeros((1, ROWS), jnp.int32)
    start = (SPAN - shard_index()) * TOK
    lens_copy.wait()
    for doc in range(lens_smem.shape[0]):
        low = jnp.where(high >= start, start, low)
        start = start + lens_smem[doc]
    low_ref[...] = low
    for copy in copies:
        copy.wait()


def load_keys(ref, slot, keys_ref, rot2_ref):
    rows = slice(slot * TOK, (slot + 1) * TOK)
    keys_ref[rows, :] = ref[0:TOK, :]
    rot_t = load_rotary(ref).astype(F32)
    rot2_ref[rows, :] = jnp.transpose(jnp.concatenate([rot_t, rot_t], axis=0)).astype(BF16)


def near_kernel(
    q_ref, qx_ref, do_ref, own_ref, k2_ref, raw_ref, prob_grad_ref, keys_ref, rot2_ref
):
    load_keys(k2_ref, 0, keys_ref, rot2_ref)
    load_keys(own_ref, 1, keys_ref, rot2_ref)
    raw_ref[...] = dot(keys_ref[...], q_ref[...], NT) + dot(rot2_ref[...], qx_ref[...], NT)
    prob_grad_ref[...] = dot(keys_ref[...], do_ref[...], NT)


def scores_kernel(
    low_ref, q_ref, qx_ref, do_ref, k1_ref, k3_ref, raw_ref, prob_grad_ref, near_ref, near2_ref,
    f3_ref, f2_ref, f1_ref, dst_ref, pt_ref, keys_ref, rot2_ref,
):
    load_keys(k3_ref, 0, keys_ref, rot2_ref)
    load_keys(k1_ref, 1, keys_ref, rot2_ref)
    keys_ref[HALF:, :] = near_ref[...]
    rot2_ref[HALF:, :] = near2_ref[...]
    low = low_ref[...]
    high = lax.broadcasted_iota(jnp.int32, (1, ROWS), 1) // HEADS + FAR
    key = lax.broadcasted_iota(jnp.int32, (TOK, CHUNK), 0)
    far = slice(0, HALF)
    for c in range(ROWS // CHUNK):
        cols = slice(c * CHUNK, (c + 1) * CHUNK)
        raw_far = dot(keys_ref[far, :], q_ref[cols, :], NT) + dot(rot2_ref[far, :], qx_ref[cols, :], NT)
        lower = low[:, cols]
        masked = jnp.concatenate(
            [
                jnp.where(key >= lower, raw_far[0:TOK], NEGATIVE),
                jnp.where(key >= lower - 2 * TOK, raw_far[TOK:], NEGATIVE),
                jnp.where(key >= lower - TOK, raw_ref[0:TOK, cols], NEGATIVE),
                jnp.where(
                    (key >= lower - FAR) & (key <= high[:, cols] - FAR), raw_ref[TOK:, cols], NEGATIVE
                ),
            ],
            axis=0,
        )
        peak = jnp.max(masked, axis=0, keepdims=True)
        terms = jnp.exp2((masked - peak) * (SCALE * LOG2_E))
        probs = terms * (1.0 / jnp.sum(terms, axis=0, keepdims=True))
        low_probs = probs.astype(BF16)
        pt_ref[:, cols] = low_probs
        prob_grad = jnp.concatenate(
            [dot(keys_ref[far, :], do_ref[cols, :], NT), prob_grad_ref[:, cols]], axis=0
        )
        delta = jnp.sum(low_probs.astype(F32) * prob_grad, axis=0, keepdims=True)
        dst_ref[:, cols] = (probs * (prob_grad - delta)).astype(BF16)

    earlier = slice(0, FAR)
    grad = SCALE * dot(dst_ref[earlier, :], q_ref[...], NN) + dot(pt_ref[earlier, :], do_ref[...], NN)
    rot = SCALE * dot(dst_ref[earlier, :], qx_ref[...], NN)
    for slot, ref in enumerate((f3_ref, f1_ref, f2_ref)):
        rows = slice(slot * TOK, (slot + 1) * TOK)
        store_tile(ref, grad[rows, :], rot[rows, :])


def fold_rotary(rot):
    rot_t = jnp.transpose(rot)
    return rot_t[0:DR, :] + rot_t[DR:, :]


def store_tile(ref, grad, rot):
    ref[0:TOK, :] = grad.astype(ref.dtype)
    store_rotary(ref, fold_rotary(rot))


def queries_kernel(
    q_ref, qx_ref, do_ref, dst_ref, pt_ref, keys_ref, rot2_ref, dq_ref, dqr_ref, g0_ref, x_ref
):
    own = slice(FAR, KEYS)
    grad = SCALE * dot(dst_ref[own, :], q_ref[...], NN) + dot(pt_ref[own, :], do_ref[...], NN)
    store_tile(g0_ref, grad, SCALE * dot(dst_ref[own, :], qx_ref[...], NN))
    for c in range(ROWS // CHUNK):
        cols = slice(c * CHUNK, (c + 1) * CHUNK)
        ds = jnp.transpose(dst_ref[:, cols])
        dq_ref[cols, :] = (SCALE * dot(ds, keys_ref[...], NN)).astype(BF16)
        x_ref[cols, :] = SCALE * dot(ds, rot2_ref[...], NN)
    for pair in range(HEADS // 2):
        even = x_ref[pl.ds(2 * pair, TOK, stride=HEADS), :]
        odd = x_ref[pl.ds(2 * pair + 1, TOK, stride=HEADS), :]
        dqr_ref[:, pair * 2 * DR : (pair + 1) * 2 * DR] = jnp.where(
            head_half((TOK, 2 * DR), 0), even, odd
        ).astype(BF16)


def total_kernel(g0_ref, r3_ref, r2_ref, r1_ref, out_ref):
    total = g0_ref[...]
    for ref in (r3_ref, r2_ref, r1_ref):
        total = total + ref[...].astype(F32)
    groups = out_ref.shape[0]
    for i in range(DL // TOK):
        piece = total[0:TOK, i * TOK : (i + 1) * TOK].reshape(groups, 2, 4, TOK)
        out_ref[:, 2 * i : 2 * i + 2, :, :] = piece.astype(BF16)
    parts = [total[TOK:, i * TOK : (i + 1) * TOK] for i in range(DL // TOK)]
    rot = jnp.transpose(jnp.concatenate(parts + parts, axis=0)).reshape(groups, 2, 4, 2 * DR)
    lane = lax.broadcasted_iota(jnp.int32, (groups, 4, 2 * DR), 2)
    out_ref[:, 2 * (DL // TOK), :, :] = jnp.where(lane < DR, rot[:, 0], rot[:, 1]).astype(BF16)


def sum_kernel(blocks_ref, lat_ref, rot_ref):
    total = jnp.sum(blocks_ref[...].astype(F32), axis=0)
    for i in range(DL // TOK):
        rows = jnp.concatenate([total[2 * i], total[2 * i + 1]], axis=0)
        lat_ref[:, i * TOK : (i + 1) * TOK] = rows.astype(BF16)
    last = total[2 * (DL // TOK)]
    rot_ref[...] = jnp.concatenate([last[:, 0:DR], last[:, DR:]], axis=0).astype(BF16)


def shape(dims, dtype=BF16):
    return jax.ShapeDtypeStruct(dims, dtype)


def call(kernel, outs, spaces, scratch=(), flops=0, moved=0, name=None, limit=24):
    return pl.pallas_call(
        kernel,
        out_shape=outs,
        in_specs=[spec(s) for s in spaces],
        out_specs=jax.tree.map(lambda _: spec(), outs),
        scratch_shapes=scratch,
        compiler_params=pltpu.CompilerParams(vmem_limit_bytes=limit << 20),
        cost_estimate=pl.CostEstimate(flops=flops, bytes_accessed=moved, transcendentals=0),
        name=name,
    )


def in_hbm(x):
    return pltpu.with_memory_space_constraint(x, pltpu.HBM)


def pack(latents, rotary_t):
    return call(
        pack_kernel, shape((PACK, DL)), [HBM] * 2,
        scratch=[pltpu.SemaphoreType.DMA((1 + DL // TOK,))], moved=300000, name="pack",
    )(latents, rotary_t)


def row_setup(lens, q, do, qr):
    outs = (shape((ROWS, DL)), shape((ROWS, DL)), shape((ROWS, 2 * DR)), shape((1, ROWS), jnp.int32))
    return call(
        rows_kernel, outs, [HBM, HBM, HBM, VMEM],
        scratch=[
            pltpu.SMEM(lens.shape, jnp.int32),
            pltpu.VMEM((ROWS, 2 * DR), F32),
            pltpu.SemaphoreType.DMA((2 * FETCHES + 1,)),
        ],
        moved=4 << 20, name="row_setup",
    )(lens, q, do, qr)


def near_scores(q, qx, do, own, k2):
    outs = (
        shape((HALF, ROWS), F32), shape((HALF, ROWS), F32), shape((HALF, DL)), shape((HALF, 2 * DR)),
    )
    return call(
        near_kernel, outs, [VMEM] * 5, flops=2 * ROWS * KEYS * DL, moved=4 << 20, name="near_scores"
    )(q, qx, do, own, k2)


def scores(low, q, qx, do, k1, k3, raw, prob_grad, near, near2):
    tile = shape((PACK, DL))
    outs = (
        tile, tile, tile, shape((KEYS, ROWS)), shape((KEYS, ROWS)),
        shape((KEYS, DL)), shape((KEYS, 2 * DR)),
    )
    return call(
        scores_kernel, outs, [VMEM] * 10,
        flops=2 * ROWS * KEYS * DL * 2, moved=6 << 20, name="scores",
    )(low, q, qx, do, k1, k3, raw, prob_grad, near, near2)


def queries(q, qx, do, dst, pt, keys, rot2):
    outs = (shape((ROWS, DL)), shape((TOK, HEADS * DR)), shape((PACK, DL), F32))
    return call(
        queries_kernel, outs, [VMEM] * 7, scratch=[pltpu.VMEM((ROWS, 2 * DR), F32)],
        flops=2 * ROWS * KEYS * DL * 2, moved=6 << 20, name="queries",
    )(q, qx, do, dst, pt, keys, rot2)


def total(g0, r3, r2, r1, groups):
    return call(
        total_kernel, shape((groups, BLOCK, 4, TOK)), [VMEM] * 4, moved=1 << 20, name="total"
    )(g0, r3, r2, r1)


def head_sum(blocks):
    rows = TOK // blocks.shape[0]
    return call(
        sum_kernel, (shape((rows, DL)), shape((rows, DR))), [VMEM], moved=200000, name="head_sum"
    )(blocks)


def shifted(block, axis, distance):
    devices = range(lax.axis_size(axis))
    route = [(i - distance, i) for i in devices if i - distance in devices]
    return lax.ppermute(block, axis, route)


def body(query_latent, query_rotary, latents, key_rotary, out_grad, doc_lengths):
    head_devices = lax.axis_size("head")
    q = query_latent.reshape(ROWS, DL)
    do = out_grad.reshape(ROWS, DL)
    own = pack(in_hbm(latents), in_hbm(key_rotary.T))
    k1, k2, k3 = [shifted(own, "tok", distance) for distance in (1, 2, 3)]
    q, do, qx, low = row_setup(in_hbm(doc_lengths), in_hbm(q), in_hbm(do), query_rotary)
    raw, prob_grad, near, near2 = near_scores(q, qx, do, own, k2)
    f3, f2, f1, dst, pt, keys, rot2 = scores(low, q, qx, do, k1, k3, raw, prob_grad, near, near2)
    r3, r2, r1 = [shifted(f, "tok", -d) for d, f in ((3, f3), (2, f2), (1, f1))]
    dq, dqr, g0 = queries(q, qx, do, dst, pt, keys, rot2)
    blocks = total(g0, r3, r2, r1, head_devices)
    blocks = lax.all_to_all(blocks, "head", split_axis=0, concat_axis=0, tiled=True)
    grad_latents, grad_key_rotary = head_sum(blocks)
    return dq.reshape(TOK, HEADS, DL), dqr, grad_latents, grad_key_rotary


def solution(mesh):
    in_specs = (
        P("tok", "head", None),
        P("tok", "head"),
        P("tok", None),
        P("tok", None),
        P("tok", "head", None),
        P(),
    )
    out_specs = (
        P("tok", "head", None),
        P("tok", "head"),
        P(("tok", "head"), None),
        P(("tok", "head"), None),
    )
    return jax.shard_map(body, mesh=mesh, in_specs=in_specs, out_specs=out_specs, check_vma=False)
```

```python
import jax
import jax.numpy as jnp
from jax import lax
from jax.experimental import pallas as pl
from jax.experimental.pallas import tpu as pltpu
from jax.sharding import PartitionSpec as P


SPAN = 3


SCALE = 0.07216878364870322
LOG2_E = 1.4426950408889634
NEGATIVE = -1e30

TOK = 128
HEADS = 8
DL = 512
DR = 64
ROWS = TOK * HEADS
KEYS = (SPAN + 1) * TOK
FAR = SPAN * TOK
PACK = TOK + TOK * DR // DL
CHUNK = 256
HALF = KEYS // 2
BLOCK = 2 * (DL // TOK) + 1
FETCHES = 4

F32 = jnp.float32
BF16 = jnp.bfloat16
VMEM = pltpu.MemorySpace.VMEM
HBM = pltpu.MemorySpace.HBM

NT = (((1,), (1,)), ((), ()))
NN = (((1,), (0,)), ((), ()))


def dot(a, b, dims):
    return lax.dot_general(a, b, dims, preferred_element_type=F32)


def spec(space=VMEM):
    return pl.BlockSpec(memory_space=space)


def store_rotary(ref, rotary_t):
    for i in range(DL // TOK):
        ref[TOK:PACK, i * TOK : (i + 1) * TOK] = rotary_t[16 * i : 16 * (i + 1), :].astype(ref.dtype)


def load_rotary(ref):
    parts = [ref[TOK:PACK, i * TOK : (i + 1) * TOK] for i in range(DL // TOK)]
    return jnp.concatenate(parts, axis=0)


def pack_kernel(lat_ref, rot_t_ref, out_ref, sems):
    copies = [pltpu.make_async_copy(lat_ref, out_ref.at[pl.ds(0, TOK), :], sems.at[0])]
    for i in range(DL // TOK):
        place = out_ref.at[pl.ds(TOK, PACK - TOK), pl.ds(i * TOK, TOK)]
        copies.append(
            pltpu.make_async_copy(rot_t_ref.at[pl.ds(16 * i, 16), :], place, sems.at[1 + i])
        )
    for copy in copies:
        copy.start()
    for copy in copies:
        copy.wait()


def head_half(shape, head):
    lane = lax.broadcasted_iota(jnp.int32, shape, 1)
    return (lane >= DR) == (head % 2 == 1)


def shard_index():
    return lax.axis_index("tok").astype(jnp.int32)


def rows_kernel(
    lens_ref, q_ref, do_ref, qr_ref, qv_ref, dov_ref, qx_ref, low_ref, lens_smem, qx32_ref, sems
):
    copies = []
    for i in range(FETCHES):
        part = pl.ds(i * ROWS // FETCHES, ROWS // FETCHES)
        copies.append(pltpu.make_async_copy(q_ref.at[part, :], qv_ref.at[part, :], sems.at[2 * i]))
        copies.append(
            pltpu.make_async_copy(do_ref.at[part, :], dov_ref.at[part, :], sems.at[2 * i + 1])
        )
    lens_copy = pltpu.make_async_copy(lens_ref, lens_smem, sems.at[2 * FETCHES])
    lens_copy.start()
    for copy in copies:
        copy.start()
    for head in range(HEADS):
        pair = qr_ref[:, (head // 2) * 2 * DR : (head // 2 + 1) * 2 * DR].astype(F32)
        qx32_ref[pl.ds(head, TOK, stride=HEADS), :] = jnp.where(
            head_half((TOK, 2 * DR), head), pair, 0.0
        )
    qx_ref[...] = qx32_ref[...].astype(BF16)
    high = lax.broadcasted_iota(jnp.int32, (1, ROWS), 1) // HEADS + FAR
    low = jnp.zeros((1, ROWS), jnp.int32)
    start = (SPAN - shard_index()) * TOK
    lens_copy.wait()
    for doc in range(lens_smem.shape[0]):
        low = jnp.where(high >= start, start, low)
        start = start + lens_smem[doc]
    low_ref[...] = low
    for copy in copies:
        copy.wait()


def load_keys(ref, slot, keys_ref, rot2_ref):
    rows = slice(slot * TOK, (slot + 1) * TOK)
    keys_ref[rows, :] = ref[0:TOK, :]
    rot_t = load_rotary(ref).astype(F32)
    rot2_ref[rows, :] = jnp.transpose(jnp.concatenate([rot_t, rot_t], axis=0)).astype(BF16)


def near_kernel(
    q_ref, qx_ref, do_ref, own_ref, k2_ref, raw_ref, prob_grad_ref, keys_ref, rot2_ref
):
    load_keys(k2_ref, 0, keys_ref, rot2_ref)
    load_keys(own_ref, 1, keys_ref, rot2_ref)
    raw_ref[...] = dot(keys_ref[...], q_ref[...], NT) + dot(rot2_ref[...], qx_ref[...], NT)
    prob_grad_ref[...] = dot(keys_ref[...], do_ref[...], NT)


def scores_kernel(
    low_ref, q_ref, qx_ref, do_ref, k1_ref, k3_ref, raw_ref, prob_grad_ref, near_ref, near2_ref,
    f3_ref, f2_ref, f1_ref, dst_ref, pt_ref, keys_ref, rot2_ref,
):
    load_keys(k3_ref, 0, keys_ref, rot2_ref)
    load_keys(k1_ref, 1, keys_ref, rot2_ref)
    keys_ref[HALF:, :] = near_ref[...]
    rot2_ref[HALF:, :] = near2_ref[...]
    low = low_ref[...]
    high = lax.broadcasted_iota(jnp.int32, (1, ROWS), 1) // HEADS + FAR
    key = lax.broadcasted_iota(jnp.int32, (TOK, CHUNK), 0)
    far = slice(0, HALF)
    for c in range(ROWS // CHUNK):
        cols = slice(c * CHUNK, (c + 1) * CHUNK)
        raw_far = dot(keys_ref[far, :], q_ref[cols, :], NT) + dot(rot2_ref[far, :], qx_ref[cols, :], NT)
        lower = low[:, cols]
        masked = jnp.concatenate(
            [
                jnp.where(key >= lower, raw_far[0:TOK], NEGATIVE),
                jnp.where(key >= lower - 2 * TOK, raw_far[TOK:], NEGATIVE),
                jnp.where(key >= lower - TOK, raw_ref[0:TOK, cols], NEGATIVE),
                jnp.where(
                    (key >= lower - FAR) & (key <= high[:, cols] - FAR), raw_ref[TOK:, cols], NEGATIVE
                ),
            ],
            axis=0,
        )
        peak = jnp.max(masked, axis=0, keepdims=True)
        terms = jnp.exp2((masked - peak) * (SCALE * LOG2_E))
        probs = terms * (1.0 / jnp.sum(terms, axis=0, keepdims=True))
        low_probs = probs.astype(BF16)
        pt_ref[:, cols] = low_probs
        prob_grad = jnp.concatenate(
            [dot(keys_ref[far, :], do_ref[cols, :], NT), prob_grad_ref[:, cols]], axis=0
        )
        delta = jnp.sum(low_probs.astype(F32) * prob_grad, axis=0, keepdims=True)
        dst_ref[:, cols] = (probs * (prob_grad - delta)).astype(BF16)

    earlier = slice(0, FAR)
    grad = SCALE * dot(dst_ref[earlier, :], q_ref[...], NN) + dot(pt_ref[earlier, :], do_ref[...], NN)
    rot = SCALE * dot(dst_ref[earlier, :], qx_ref[...], NN)
    for slot, ref in enumerate((f3_ref, f1_ref, f2_ref)):
        rows = slice(slot * TOK, (slot + 1) * TOK)
        store_tile(ref, grad[rows, :], rot[rows, :])


def fold_rotary(rot):
    rot_t = jnp.transpose(rot)
    return rot_t[0:DR, :] + rot_t[DR:, :]


def store_tile(ref, grad, rot):
    ref[0:TOK, :] = grad.astype(ref.dtype)
    store_rotary(ref, fold_rotary(rot))


def queries_kernel(
    q_ref, qx_ref, do_ref, dst_ref, pt_ref, keys_ref, rot2_ref, dq_ref, dqr_ref, g0_ref, x_ref
):
    own = slice(FAR, KEYS)
    grad = SCALE * dot(dst_ref[own, :], q_ref[...], NN) + dot(pt_ref[own, :], do_ref[...], NN)
    store_tile(g0_ref, grad, SCALE * dot(dst_ref[own, :], qx_ref[...], NN))
    for c in range(ROWS // CHUNK):
        cols = slice(c * CHUNK, (c + 1) * CHUNK)
        ds = jnp.transpose(dst_ref[:, cols])
        dq_ref[cols, :] = (SCALE * dot(ds, keys_ref[...], NN)).astype(BF16)
        x_ref[cols, :] = SCALE * dot(ds, rot2_ref[...], NN)
    for pair in range(HEADS // 2):
        even = x_ref[pl.ds(2 * pair, TOK, stride=HEADS), :]
        odd = x_ref[pl.ds(2 * pair + 1, TOK, stride=HEADS), :]
        dqr_ref[:, pair * 2 * DR : (pair + 1) * 2 * DR] = jnp.where(
            head_half((TOK, 2 * DR), 0), even, odd
        ).astype(BF16)


def total_kernel(g0_ref, r3_ref, r2_ref, r1_ref, out_ref):
    total = g0_ref[...]
    for ref in (r3_ref, r2_ref, r1_ref):
        total = total + ref[...].astype(F32)
    groups = out_ref.shape[0]
    for i in range(DL // TOK):
        piece = total[0:TOK, i * TOK : (i + 1) * TOK].reshape(groups, 2, 4, TOK)
        out_ref[:, 2 * i : 2 * i + 2, :, :] = piece.astype(BF16)
    parts = [total[TOK:, i * TOK : (i + 1) * TOK] for i in range(DL // TOK)]
    rot = jnp.transpose(jnp.concatenate(parts + parts, axis=0)).reshape(groups, 2, 4, 2 * DR)
    lane = lax.broadcasted_iota(jnp.int32, (groups, 4, 2 * DR), 2)
    out_ref[:, 2 * (DL // TOK), :, :] = jnp.where(lane < DR, rot[:, 0], rot[:, 1]).astype(BF16)


def sum_kernel(blocks_ref, lat_ref, rot_ref):
    total = jnp.sum(blocks_ref[...].astype(F32), axis=0)
    for i in range(DL // TOK):
        rows = jnp.concatenate([total[2 * i], total[2 * i + 1]], axis=0)
        lat_ref[:, i * TOK : (i + 1) * TOK] = rows.astype(BF16)
    last = total[2 * (DL // TOK)]
    rot_ref[...] = jnp.concatenate([last[:, 0:DR], last[:, DR:]], axis=0).astype(BF16)


def shape(dims, dtype=BF16):
    return jax.ShapeDtypeStruct(dims, dtype)


def call(kernel, outs, spaces, scratch=(), flops=0, moved=0, limit=24):
    return pl.pallas_call(
        kernel,
        out_shape=outs,
        in_specs=[spec(s) for s in spaces],
        out_specs=jax.tree.map(lambda _: spec(), outs),
        scratch_shapes=scratch,
        compiler_params=pltpu.CompilerParams(vmem_limit_bytes=limit << 20),
        cost_estimate=pl.CostEstimate(flops=flops, bytes_accessed=moved, transcendentals=0),
    )


def in_hbm(x):
    return pltpu.with_memory_space_constraint(x, pltpu.HBM)


def pack(latents, rotary_t):
    return call(
        pack_kernel, shape((PACK, DL)), [HBM] * 2,
        scratch=[pltpu.SemaphoreType.DMA((1 + DL // TOK,))], moved=300000,
    )(latents, rotary_t)


def row_setup(lens, q, do, qr):
    outs = (shape((ROWS, DL)), shape((ROWS, DL)), shape((ROWS, 2 * DR)), shape((1, ROWS), jnp.int32))
    return call(
        rows_kernel, outs, [HBM, HBM, HBM, VMEM],
        scratch=[
            pltpu.SMEM(lens.shape, jnp.int32),
            pltpu.VMEM((ROWS, 2 * DR), F32),
            pltpu.SemaphoreType.DMA((2 * FETCHES + 1,)),
        ],
        moved=4 << 20,
    )(lens, q, do, qr)


def near_scores(q, qx, do, own, k2):
    outs = (
        shape((HALF, ROWS), F32), shape((HALF, ROWS), F32), shape((HALF, DL)), shape((HALF, 2 * DR)),
    )
    return call(near_kernel, outs, [VMEM] * 5, flops=2 * ROWS * KEYS * DL, moved=4 << 20)(q, qx, do, own, k2)


def scores(low, q, qx, do, k1, k3, raw, prob_grad, near, near2):
    tile = shape((PACK, DL))
    outs = (
        tile, tile, tile, shape((KEYS, ROWS)), shape((KEYS, ROWS)),
        shape((KEYS, DL)), shape((KEYS, 2 * DR)),
    )
    return call(
        scores_kernel, outs, [VMEM] * 10,
        flops=2 * ROWS * KEYS * DL * 2, moved=6 << 20,
    )(low, q, qx, do, k1, k3, raw, prob_grad, near, near2)


def queries(q, qx, do, dst, pt, keys, rot2):
    outs = (shape((ROWS, DL)), shape((TOK, HEADS * DR)), shape((PACK, DL), F32))
    return call(
        queries_kernel, outs, [VMEM] * 7, scratch=[pltpu.VMEM((ROWS, 2 * DR), F32)],
        flops=2 * ROWS * KEYS * DL * 2, moved=6 << 20,
    )(q, qx, do, dst, pt, keys, rot2)


def total(g0, r3, r2, r1, groups):
    return call(total_kernel, shape((groups, BLOCK, 4, TOK)), [VMEM] * 4, moved=1 << 20)(g0, r3, r2, r1)


def head_sum(blocks):
    rows = TOK // blocks.shape[0]
    return call(sum_kernel, (shape((rows, DL)), shape((rows, DR))), [VMEM], moved=200000)(blocks)


def shifted(block, axis, distance):
    devices = range(lax.axis_size(axis))
    route = [(i - distance, i) for i in devices if i - distance in devices]
    return lax.ppermute(block, axis, route)


def body(query_latent, query_rotary, latents, key_rotary, out_grad, doc_lengths):
    head_devices = lax.axis_size("head")
    q = query_latent.reshape(ROWS, DL)
    do = out_grad.reshape(ROWS, DL)
    own = pack(in_hbm(latents), in_hbm(key_rotary.T))
    fetched = []
    for distance in (1, 2, 3):
        fetched.append(shifted(own, "tok", distance))
    k1, k2, k3 = fetched
    q, do, qx, low = row_setup(in_hbm(doc_lengths), in_hbm(q), in_hbm(do), query_rotary)
    raw, prob_grad, near, near2 = near_scores(q, qx, do, own, k2)
    f3, f2, f1, dst, pt, keys, rot2 = scores(low, q, qx, do, k1, k3, raw, prob_grad, near, near2)
    r3, r2, r1 = [shifted(f, "tok", -d) for d, f in ((3, f3), (2, f2), (1, f1))]
    dq, dqr, g0 = queries(q, qx, do, dst, pt, keys, rot2)
    blocks = total(g0, r3, r2, r1, head_devices)
    blocks = lax.all_to_all(blocks, "head", split_axis=0, concat_axis=0, tiled=True)
    grad_latents, grad_key_rotary = head_sum(blocks)
    return dq.reshape(TOK, HEADS, DL), dqr, grad_latents, grad_key_rotary


def solution(mesh):
    in_specs = (
        P("tok", "head", None),
        P("tok", "head"),
        P("tok", None),
        P("tok", None),
        P("tok", "head", None),
        P(),
    )
    out_specs = (
        P("tok", "head", None),
        P("tok", "head"),
        P(("tok", "head"), None),
        P(("tok", "head"), None),
    )
    return jax.shard_map(body, mesh=mesh, in_specs=in_specs, out_specs=out_specs, check_vma=False)
```
